32 devices in a mesh: group: 2 (over x), rep: 16 (over z, y, core).
Axes of the slice: x: 2, y: 2, z: 4, core: 2. Of those that a mesh axis runs over, the one named last changes fastest.
Arguments:
- queries: bfloat16 [4096, 4096], P(('group', 'rep')), parts along dimension 0
- prompt_keys: bfloat16 [4096, 512], P(('group', 'rep')), parts along dimension 0
- prompt_value_rows: bfloat16 [4096, 512], P(('group', 'rep')), parts along dimension 0, may hold values from -6 to 6
- document_keys: bfloat16 [16384, 512], P(('group', 'rep')), parts along dimension 0, may hold values from -12 to 12
- document_values: bfloat16 [16384, 512], P(('group', 'rep')), parts along dimension 0, may hold values from -6 to 6
- span_owner: int32 [32], P('group'), parts along dimension 0, may hold values from 0 to 15, each once
- block_list: int32 [32, 8], P(('group', 'rep')), parts along dimension 0, may hold values from 0 to 63, as said below
- prompt_length: int32 [32], P(('group', 'rep')), parts along dimension 0, may hold values from 2 to 128
Outputs:
- attended: bfloat16 [4096, 4096], P(('group', 'rep')), parts along dimension 0
The draws below stay inside these ranges and needn't reach their ends.
There are 2 independent parts, one for each index of `group`. The reference program is written for one: setup_inputs(seed, part) draws one part's arguments, and reference() takes and returns one part's arrays. A program takes and returns all parts, laid end to end along the dimension named above; each array names one. Nothing has to cross between parts.
Inputs may be any that keep to these rules, and one draw needn't show every extreme that they name: Each replica holds exactly one span: span_owner is a permutation. `block_list`: the 8 blocks listed by one replica lie in 8 different spans.
All inputs are finite; a program needn't handle non-finite values.
Results may differ from the reference program's by a relative error of at most 0.0049.
Values may be sent and summed in bfloat16 or wider, within the bound.
No kernel may reach another device: no remote copies, remote signals or barrier semaphores. Data moves between devices by JAX's collectives and lax.ppermute only.
A program may use at most 128 MiB of HBM per device.

```python
import jax
import jax.numpy as jnp
from jax import lax

QUERY_HEADS = 32
KEY_VALUE_HEADS = 4
HEAD_SIZE = 128
BLK = 128
PBLK = 1
SPAN_BLK = 4
LIST = 8
PROMPT_SLOTS = 2048
DOCUMENT_TOKENS = 8192
N_REP = 16


def draw_queries(key, part):
    row_total = N_REP * PBLK * BLK
    value_matrix = jax.random.normal(jax.random.fold_in(key, 1), (row_total, QUERY_HEADS * HEAD_SIZE), jnp.float32)
    value_matrix = jnp.clip(value_matrix, -6.0, 6.0)
    return value_matrix.astype(jnp.bfloat16)


def draw_prompt_keys(key, part):
    row_total = N_REP * PBLK * BLK
    value_matrix = 2.0 * jax.random.normal(jax.random.fold_in(key, 3), (row_total, KEY_VALUE_HEADS * HEAD_SIZE), jnp.float32)
    value_matrix = jnp.clip(value_matrix, -12.0, 12.0)
    return value_matrix.astype(jnp.bfloat16)


def draw_block_list(key, part):
    random_jitter = jax.random.randint(jax.random.fold_in(key, 11), (N_REP, N_REP), 0, 1 << 14)
    extra_reward = jax.random.randint(jax.random.fold_in(key, 12), (N_REP,), 0, 4) * (1 << 14)
    logit_score = random_jitter + extra_reward[None, :]
    logit_score = logit_score.at[0, 0].add(1 << 17).at[0, N_REP - 1].add(1 << 17)
    keyed = logit_score * N_REP + jnp.arange(N_REP, dtype=jnp.int32)[None, :]
    top_values, spans = lax.top_k(keyed, LIST)
    inner = jax.random.randint(jax.random.fold_in(key, 13), (N_REP, LIST), 0, SPAN_BLK)
    first_row = (jnp.arange(N_REP, dtype=jnp.int32) == 0)[:, None]
    inner = jnp.where(first_row & (spans == 0), 0, inner)
    inner = jnp.where(first_row & (spans == N_REP - 1), SPAN_BLK - 1, inner)
    return (spans * SPAN_BLK + inner).astype(jnp.int32)


def draw_prompt_length(key, part):
    lengths = jax.random.randint(jax.random.fold_in(key, 21), (N_REP,), 2, PBLK * BLK + 1)
    longest = jax.random.randint(jax.random.fold_in(key, 22), (), 0, N_REP)
    shortest = (longest + 1 + jax.random.randint(jax.random.fold_in(key, 23), (), 0, N_REP - 1)) % N_REP
    lengths = lengths.at[longest].set(PBLK * BLK).at[shortest].set(2)
    return lengths.astype(jnp.int32)


def levels(own_key, shape, split, least, top_value):
    loudness, own = 1.0, jax.random.fold_in(own_key, 6)
    for dim, shards_of in split:
        steps = jnp.exp(jax.random.uniform(jax.random.fold_in(own, dim), (shards_of,), jnp.float32, least / len(split), top_value / len(split)))
        loudness = loudness * jnp.repeat(steps, shape[dim] // shards_of).reshape([-1 if axis == dim else 1 for axis in range(len(shape))])
    return loudness


def centred(own_key, extent, spread, most, split=(), kind=jnp.bfloat16):
    drawn = spread * jax.random.normal(own_key, extent, jnp.float32)
    if split:
        drawn = drawn * levels(own_key, extent, split, -0.22, 0.18)
    return jnp.clip(drawn, -most, most).astype(kind)


def setup_inputs(seed: int = 0, part: int = 0) -> dict:
    splits = jax.random.split(jax.random.key(seed), 9)
    part_keys = jax.random.split(jax.random.fold_in(splits[8], part), 9)
    queries = draw_queries(jax.random.fold_in(jax.random.fold_in(splits[8], part), 71), part)
    prompt_keys = draw_prompt_keys(jax.random.fold_in(jax.random.fold_in(splits[8], part), 71), part)
    prompt_value_rows = centred(part_keys[2], (PROMPT_SLOTS, KEY_VALUE_HEADS * HEAD_SIZE), 1.0, 6.0, ((0, 16),))
    document_keys = centred(part_keys[3], (DOCUMENT_TOKENS, KEY_VALUE_HEADS * HEAD_SIZE), 2.0, 12.0, ((0, 16),))
    document_values = centred(part_keys[4], (DOCUMENT_TOKENS, KEY_VALUE_HEADS * HEAD_SIZE), 1.0, 6.0, ((0, 16),))
    span_owner = jax.random.permutation(part_keys[5], N_REP).astype(jnp.int32)
    block_list = draw_block_list(jax.random.fold_in(jax.random.fold_in(splits[8], part), 71), part)
    prompt_length = draw_prompt_length(jax.random.fold_in(jax.random.fold_in(splits[8], part), 71), part)
    return dict(queries=queries, prompt_keys=prompt_keys, prompt_value_rows=prompt_value_rows, document_keys=document_keys, document_values=document_values, span_owner=span_owner, block_list=block_list, prompt_length=prompt_length)


def softmax_rows(query_part, key_part, visible):
    scores = jnp.einsum("thd,kd->htk", query_part.astype(jnp.float32), key_part.astype(jnp.float32), precision=lax.Precision.HIGHEST) * (HEAD_SIZE ** -0.5)
    scores = jnp.where(visible[None], scores, -jnp.inf)
    largest = jnp.max(scores, axis=-1, keepdims=True)
    weights = jnp.exp(scores - largest)
    return (weights / jnp.sum(weights, axis=-1, keepdims=True)).astype(jnp.bfloat16)


def reference(queries, prompt_keys, prompt_value_rows, document_keys, document_values, span_owner, block_list, prompt_length):
    rows_each = PBLK * BLK
    group_width = QUERY_HEADS // KEY_VALUE_HEADS

    def one_replica(rank):
        query_rows = lax.dynamic_slice_in_dim(queries, rank * rows_each, rows_each, 0)
        own_keys = lax.dynamic_slice_in_dim(prompt_keys, rank * rows_each, rows_each, 0)
        own_values = lax.dynamic_slice_in_dim(prompt_value_rows, rank * rows_each, rows_each, 0)
        listed = lax.dynamic_index_in_dim(block_list, rank, 0, keepdims=False)
        holder = jnp.take(span_owner, listed // SPAN_BLK, axis=0)
        starts = (holder * SPAN_BLK + listed % SPAN_BLK) * BLK
        row_index = (starts[:, None] + jnp.arange(BLK, dtype=jnp.int32)[None, :]).reshape(-1).astype(jnp.int32)
        keys_all = jnp.concatenate([jnp.take(document_keys, row_index, axis=0), own_keys], axis=0)
        values_all = jnp.concatenate([jnp.take(document_values, row_index, axis=0), own_values], axis=0)
        doc_count = LIST * BLK
        positions = jnp.arange(rows_each, dtype=jnp.int32)
        key_slots = jnp.arange(doc_count + rows_each, dtype=jnp.int32) - doc_count
        visible = key_slots[None, :] <= positions[:, None]
        pieces = []
        for head_cluster in range(KEY_VALUE_HEADS):
            cols = slice(head_cluster * group_width * HEAD_SIZE, (head_cluster + 1) * group_width * HEAD_SIZE)
            query_part = query_rows[:, cols].reshape(rows_each, group_width, HEAD_SIZE)
            probs = softmax_rows(query_part, keys_all[:, head_cluster * HEAD_SIZE:(head_cluster + 1) * HEAD_SIZE], visible)
            mixed = jnp.einsum("htk,kd->thd", probs.astype(jnp.float32), values_all[:, head_cluster * HEAD_SIZE:(head_cluster + 1) * HEAD_SIZE].astype(jnp.float32), precision=lax.Precision.HIGHEST)
            pieces.append(mixed.reshape(rows_each, group_width * HEAD_SIZE))
        joined = jnp.concatenate(pieces, axis=1).astype(jnp.bfloat16)
        length = lax.dynamic_index_in_dim(prompt_length, rank, 0, keepdims=False)
        live = positions < length
        return jnp.where(live[:, None], joined, jnp.zeros_like(joined))

    result = lax.map(one_replica, jnp.arange(N_REP, dtype=jnp.int32))
    return result.reshape(N_REP * rows_each, QUERY_HEADS * HEAD_SIZE)
```

```python
import math

import jax
import jax.numpy as jnp
from jax import lax
from jax.experimental import pallas as pl
from jax.experimental.pallas import tpu as pltpu
from jax.sharding import PartitionSpec as P

QUERY_HEADS = 32
KEY_VALUE_HEADS = 4
HEAD_SIZE = 128
BLK = 128
SPAN_BLK = 4
LIST = 8
GROUP = QUERY_HEADS // KEY_VALUE_HEADS
HALF_HEADS = KEY_VALUE_HEADS // 2
HALF_KV = HALF_HEADS * HEAD_SIZE
HALF_Q = HALF_HEADS * GROUP * HEAD_SIZE
SCALE2 = math.log2(math.e) / math.sqrt(HEAD_SIZE)
NKEYS = (LIST + 1) * BLK


SMEM = pl.BlockSpec(memory_space=pltpu.SMEM)
VMEM = pl.BlockSpec(memory_space=pltpu.VMEM)
ANY = pl.BlockSpec(memory_space=pl.ANY)


def rank_pairs(move):
    pairs = []
    for z in range(4):
        for y in range(2):
            for c in range(2):
                to = move(z, y, c)
                if to is not None:
                    pairs.append((z * 4 + y * 2 + c, to[0] * 4 + to[1] * 2 + to[2]))
    return pairs


CORE = rank_pairs(lambda z, y, c: (z, y, 1 - c))
SIDE = rank_pairs(lambda z, y, c: (z, 1 - y, c))
MID_SIDE = rank_pairs(lambda z, y, c: (z, 1 - y, c) if z in (1, 2) else None)
OUTER = rank_pairs(lambda z, y, c: (z ^ 1, y, c))
INNER = rank_pairs(lambda z, y, c: (3 - z, y, c) if z in (1, 2) else None)
END = rank_pairs(lambda z, y, c: (z ^ 1, y, c) if z in (1, 2) else None)
END_SIDE = rank_pairs(lambda z, y, c: (z ^ 1, 1 - y, c) if z in (1, 2) else None)


def hop(x, pairs):
    return lax.ppermute(x, "rep", pairs)


def place():
    rank = lax.axis_index("rep")
    return rank // 4, (rank // 2) % 2, rank % 2


def slot_kernel(plane_of, dests, owner_ref, *refs):
    lists = refs[:dests]
    same_ref, other_ref = refs[dests], refs[dests + 1]
    outs = refs[dests + 2 : 2 * dests + 2]
    sems = refs[2 * dests + 2]
    z, y, c = place()
    rank_same = plane_of(z) * 4 + y * 2 + c
    rank_other = plane_of(z) * 4 + y * 2 + 1 - c
    copies = []
    for t in range(dests):
        for d in range(2):
            at = [jnp.int32(0), jnp.int32(0)]
            for j in range(LIST):
                block = lists[t][d, j]
                owner = owner_ref[block // SPAN_BLK]
                at[0] = jnp.where(owner == rank_same, block % SPAN_BLK, at[0])
                at[1] = jnp.where(owner == rank_other, block % SPAN_BLK, at[1])
            for rel, source in enumerate((same_ref, other_ref)):
                copy = pltpu.make_async_copy(
                    source.at[at[rel]], outs[t].at[d * 2 + rel], sems.at[t * 4 + d * 2 + rel]
                )
                copy.start()
                copies.append(copy)
    for copy in copies:
        copy.wait()


def slots(plane_of, owner, lists, same, other):
    dests = len(lists)
    shape = jax.ShapeDtypeStruct((4, BLK, 2 * HALF_KV), jnp.bfloat16)
    size = dests * 4 * BLK * 2 * HALF_KV * 2
    return pl.pallas_call(
        lambda *refs: slot_kernel(plane_of, dests, *refs),
        out_shape=[shape] * dests,
        in_specs=[SMEM] * (1 + dests) + [ANY] * 2,
        out_specs=[VMEM] * dests,
        scratch_shapes=[pltpu.SemaphoreType.DMA((4 * dests,))],
        cost_estimate=pl.CostEstimate(flops=0, bytes_accessed=2 * size, transcendentals=0),
        compiler_params=pltpu.CompilerParams(vmem_limit_bytes=8 << 20),
    )(owner, *lists, same.reshape(shape.shape), other.reshape(shape.shape))


def attend_kernel(owner_ref, list_ref, q_ref, pair_q_ref, kp_ref, vp_ref, pair_kv_ref, *refs):
    sources = refs[:16]
    out_refs = refs[16:18]
    held, s_ref, p_ref, sems = refs[18:]
    z, y, c = place()
    near = z ^ 1
    mid = jnp.logical_or(z == 1, z == 2)
    inner = jnp.where(mid, 3 - z, 3 - near)

    for d in range(2):

        def fetch(j, carry, d=d):
            block = list_ref[d, j]
            owner = owner_ref[block // SPAN_BLK]
            oz, oy, oc = owner // 4, (owner // 2) % 2, owner % 2
            rel = (oc != c).astype(jnp.int32)
            level = jnp.where(oz == z, 0, jnp.where(oz == near, 1, jnp.where(oz == inner, 2, 3)))
            own_column = oy == y
            whole = jnp.logical_and(own_column, jnp.logical_or(level < 2, mid))
            spot = jnp.where(whole, block % SPAN_BLK, d * 2 + rel)
            kind = jnp.where(
                whole,
                level * 2 + rel,
                jnp.where(
                    jnp.logical_or(level < 2, mid),
                    8 + level,
                    12 + (level - 2) * 2 + jnp.where(own_column, 0, 1),
                ),
            )
            for at, source in enumerate(sources):

                @pl.when(kind == at)
                def _():
                    pltpu.make_async_copy(source.at[spot], held.at[d, j], sems.at[d, j]).start()

            return carry

        lax.fori_loop(0, LIST, fetch, 0)

    off = pl.multiple_of(c * HALF_KV, HALF_KV)
    held[0, LIST, :, :HALF_KV] = kp_ref[:, pl.ds(off, HALF_KV)]
    held[0, LIST, :, HALF_KV:] = vp_ref[:, pl.ds(off, HALF_KV)]
    held[1, LIST] = pair_kv_ref[...]
    row = lax.broadcasted_iota(jnp.int32, (BLK, BLK), 0)
    seen = lax.broadcasted_iota(jnp.int32, (BLK, BLK), 1) <= row
    for d in range(2):
        for j in range(LIST):
            pltpu.make_async_copy(sources[0].at[0], held.at[d, j], sems.at[d, j]).wait()
        for g in range(HALF_HEADS):
            keys = held[d, :, :, g * HEAD_SIZE : (g + 1) * HEAD_SIZE].reshape(NKEYS, HEAD_SIZE)
            vals = held[
                d, :, :, HALF_KV + g * HEAD_SIZE : HALF_KV + (g + 1) * HEAD_SIZE
            ].reshape(NKEYS, HEAD_SIZE)
            heads = []
            for h in range(GROUP):
                at = (g * GROUP + h) * HEAD_SIZE
                if d == 0:
                    start = pl.multiple_of(c * HALF_Q + at, HEAD_SIZE)
                    heads.append(q_ref[:, pl.ds(start, HEAD_SIZE)])
                else:
                    heads.append(pair_q_ref[:, at : at + HEAD_SIZE])
            s_ref[...] = lax.dot_general(
                jnp.concatenate(heads, axis=0),
                keys,
                (((1,), (1,)), ((), ())),
                preferred_element_type=jnp.float32,
            )
            totals = []
            for h in range(GROUP):
                rows = slice(h * BLK, (h + 1) * BLK)
                last = jnp.where(seen, s_ref[rows, LIST * BLK :], -jnp.inf)
                top = last
                for j in range(LIST):
                    top = jnp.maximum(top, s_ref[rows, j * BLK : (j + 1) * BLK])
                top = jnp.max(top, axis=1, keepdims=True)
                total = None
                for j in range(LIST + 1):
                    part = last if j == LIST else s_ref[rows, j * BLK : (j + 1) * BLK]
                    weight = jnp.exp2((part - top) * SCALE2)
                    total = weight if total is None else total + weight
                    p_ref[rows, j * BLK : (j + 1) * BLK] = weight.astype(jnp.bfloat16)
                totals.append(jnp.sum(total, axis=1, keepdims=True))
            mixed = lax.dot_general(
                p_ref[...], vals, (((1,), (0,)), ((), ())), preferred_element_type=jnp.float32
            )
            for h in range(GROUP):
                at = (g * GROUP + h) * HEAD_SIZE
                out_refs[d][:, at : at + HEAD_SIZE] = (
                    mixed[h * BLK : (h + 1) * BLK, :] / totals[h]
                ).astype(jnp.bfloat16)


def attend(owner, lists, queries, pair_q, prompt_keys, prompt_values, pair_kv, sources):
    shape = jax.ShapeDtypeStruct((BLK, HALF_Q), jnp.bfloat16)
    return pl.pallas_call(
        attend_kernel,
        out_shape=[shape] * 2,
        in_specs=[SMEM] * 2 + [VMEM] * 5 + [ANY] * 16,
        out_specs=[VMEM] * 2,
        scratch_shapes=[
            pltpu.VMEM((2, LIST + 1, BLK, 2 * HALF_KV), jnp.bfloat16),
            pltpu.VMEM((GROUP * BLK, NKEYS), jnp.float32),
            pltpu.VMEM((GROUP * BLK, NKEYS), jnp.bfloat16),
            pltpu.SemaphoreType.DMA((2, LIST)),
        ],
        cost_estimate=pl.CostEstimate(
            flops=4 * QUERY_HEADS * BLK * NKEYS * HEAD_SIZE,
            bytes_accessed=8 << 20,
            transcendentals=QUERY_HEADS * BLK * NKEYS,
        ),
        compiler_params=pltpu.CompilerParams(vmem_limit_bytes=30 << 20),
    )(
        owner,
        lists,
        queries,
        pair_q,
        prompt_keys,
        prompt_values,
        pair_kv,
        *[x.reshape(4, BLK, 2 * HALF_KV) for x in sources],
    )


def line_device(
    queries,
    prompt_keys,
    prompt_value_rows,
    document_keys,
    document_values,
    span_owner,
    block_list,
    prompt_length,
):
    first = lax.axis_index("rep") % 2 == 0

    def half(x, mine):
        width = x.shape[1] // 2
        return jnp.where(first == mine, x[:, :width], x[:, width:])

    def paired(keys, values, mine):
        return jnp.concatenate([half(keys, mine), half(values, mine)], axis=1)

    own_s = paired(document_keys, document_values, True)
    own_o = hop(paired(document_keys, document_values, False), CORE)
    outer_s = hop(own_s, OUTER)
    inner_s = hop(own_s, INNER)
    outer_o = hop(own_o, OUTER)
    inner_o = hop(own_o, INNER)

    lists = jnp.concatenate([block_list, hop(block_list, CORE)], axis=0)
    side_lists = hop(lists, SIDE)
    end_lists = hop(jnp.concatenate([lists, side_lists], axis=0), OUTER)
    pair_q = hop(half(queries, False), CORE)
    pair_kv = hop(paired(prompt_keys, prompt_value_rows, False), CORE)

    far_s = hop(outer_s, INNER)
    far_o = hop(outer_o, INNER)

    (side0,) = slots(lambda z: z, span_owner, [side_lists], own_s, own_o)
    side0 = hop(side0, SIDE)
    (side1,) = slots(lambda z: z ^ 1, span_owner, [side_lists], outer_s, outer_o)
    side1 = hop(side1, SIDE)
    dests = [end_lists[:2], end_lists[2:], side_lists]
    end2, end_side2, side2 = slots(lambda z: 3 - z, span_owner, dests, inner_s, inner_o)
    end2, end_side2 = hop(end2, END), hop(end_side2, END_SIDE)
    side2 = hop(side2, MID_SIDE)
    end3, end_side3, side3 = slots(lambda z: (3 - z) ^ 1, span_owner, dests, far_s, far_o)
    end3, end_side3 = hop(end3, END), hop(end_side3, END_SIDE)
    side3 = hop(side3, MID_SIDE)

    mine, theirs = attend(
        span_owner,
        lists,
        queries,
        pair_q,
        prompt_keys,
        prompt_value_rows,
        pair_kv,
        [own_s, own_o, outer_s, outer_o, inner_s, inner_o, far_s, far_o]
        + [side0, side1, side2, side3, end2, end_side2, end3, end_side3],
    )
    theirs = hop(theirs, CORE)
    joined = jnp.where(
        first,
        jnp.concatenate([mine, theirs], axis=1),
        jnp.concatenate([theirs, mine], axis=1),
    )
    live = jnp.arange(BLK, dtype=jnp.int32) < prompt_length[0]
    return jnp.where(live[:, None], joined, jnp.zeros_like(joined))


def probs_of(query_part, key_part, visible):
    scores = jnp.einsum(
        "thd,kd->htk", query_part, key_part, preferred_element_type=jnp.float32
    ) * query_part.shape[-1] ** (-0.5)
    scores = jnp.where(visible[None], scores, -jnp.inf)
    largest = jnp.max(scores, axis=-1, keepdims=True)
    weights = jnp.exp(scores - largest)
    return (weights / jnp.sum(weights, axis=-1, keepdims=True)).astype(jnp.bfloat16)


def per_device(
    queries,
    prompt_keys,
    prompt_value_rows,
    document_keys,
    document_values,
    span_owner,
    block_list,
    prompt_length,
):
    group_width = QUERY_HEADS // KEY_VALUE_HEADS
    count = lax.axis_size("rep")
    list_len = block_list.shape[1]
    all_ranks = jnp.arange(count, dtype=jnp.int32)
    my_list = block_list[0]
    list_span = my_list // SPAN_BLK
    owners = jnp.sum(
        jnp.where(list_span[:, None] == all_ranks[None, :], span_owner[None, :], 0), axis=1
    )
    matches = owners[None, :] == all_ranks[:, None]
    request = jnp.sum(jnp.where(matches, (my_list % SPAN_BLK + 1)[None, :], 0), axis=1) - 1
    arrived = lax.all_to_all(request, "rep", split_axis=0, concat_axis=0, tiled=True)
    wanted = arrived >= 0
    inner_block = jnp.maximum(arrived, 0)

    def outgoing(source):
        blocks = source.reshape(SPAN_BLK, BLK, source.shape[1])
        picked = jnp.take(blocks, inner_block, axis=0)
        return jnp.where(wanted[:, None, None], picked, jnp.zeros_like(picked))

    def listed(received):
        return jnp.take(received, owners, axis=0).reshape(list_len * BLK, received.shape[2])

    send_keys = outgoing(document_keys)
    send_values = outgoing(document_values)
    doc_visible = jnp.ones((BLK, list_len * BLK), dtype=bool)
    got_keys, got_values = (
        lax.all_to_all(send_keys, "rep", split_axis=0, concat_axis=0, tiled=True),
        lax.all_to_all(send_values, "rep", split_axis=0, concat_axis=0, tiled=True),
    )
    query_block = 0
    seen = (query_block + 1) * BLK
    key_rows = jnp.concatenate([listed(got_keys), prompt_keys], axis=0)
    slots = jnp.arange(seen, dtype=jnp.int32)
    positions = query_block * BLK + jnp.arange(BLK, dtype=jnp.int32)
    visible = jnp.concatenate([doc_visible, slots[None, :] <= positions[:, None]], axis=1)
    row_probs = []
    for all_head_cluster in range(KEY_VALUE_HEADS):
        cols = slice(
            all_head_cluster * group_width * HEAD_SIZE,
            (all_head_cluster + 1) * group_width * HEAD_SIZE,
        )
        query_part = queries[query_block * BLK : seen, cols].reshape(BLK, group_width, HEAD_SIZE)
        row_probs.append(
            probs_of(
                query_part,
                key_rows[:, all_head_cluster * HEAD_SIZE : (all_head_cluster + 1) * HEAD_SIZE],
                visible,
            )
        )
    table = [row_probs]
    doc_value_rows = listed(got_values)
    live_rows = prompt_length[0]
    query_block = 0
    value_rows = jnp.concatenate([doc_value_rows, prompt_value_rows], axis=0)
    pieces = []
    for head_cluster in range(KEY_VALUE_HEADS):
        mixed = jnp.einsum(
            "htk,kd->thd",
            table[query_block][head_cluster],
            value_rows[:, head_cluster * HEAD_SIZE : (head_cluster + 1) * HEAD_SIZE],
            preferred_element_type=jnp.float32,
        )
        pieces.append(mixed.reshape(BLK, group_width * HEAD_SIZE))
    joined = jnp.concatenate(pieces, axis=1).astype(jnp.bfloat16)
    positions = query_block * BLK + jnp.arange(BLK, dtype=jnp.int32)
    outputs = jnp.where((positions < live_rows)[:, None], joined, jnp.zeros_like(joined))
    return outputs


def solution(mesh):
    body = line_device if mesh.shape["rep"] == 16 else per_device
    return jax.shard_map(
        body,
        mesh=mesh,
        in_specs=(
            P(("group", "rep"), None),
            P(("group", "rep"), None),
            P(("group", "rep"), None),
            P(("group", "rep"), None),
            P(("group", "rep"), None),
            P("group"),
            P(("group", "rep"), None),
            P(("group", "rep")),
        ),
        out_specs=P(("group", "rep"), None),
        check_vma=False,
    )
```

```python
import functools
import math

import jax
import jax.numpy as jnp
from jax import lax
from jax.experimental import pallas as pl
from jax.experimental.pallas import tpu as pltpu
from jax.sharding import PartitionSpec as P

QUERY_HEADS = 32
KEY_VALUE_HEADS = 4
HEAD_SIZE = 128
BLK = 128
SPAN_BLK = 4
LIST = 8
GROUP = QUERY_HEADS // KEY_VALUE_HEADS
HALF_HEADS = KEY_VALUE_HEADS // 2
HALF_KV = HALF_HEADS * HEAD_SIZE
HALF_Q = HALF_HEADS * GROUP * HEAD_SIZE
SCALE2 = math.log2(math.e) / math.sqrt(HEAD_SIZE)


SMEM = pl.BlockSpec(memory_space=pltpu.SMEM)
VMEM = pl.BlockSpec(memory_space=pltpu.VMEM)
ANY = pl.BlockSpec(memory_space=pl.ANY)


def rank_pairs(move):
    pairs = []
    for z in range(4):
        for y in range(2):
            for c in range(2):
                to = move(z, y, c)
                if to is not None:
                    pairs.append((z * 4 + y * 2 + c, to[0] * 4 + to[1] * 2 + to[2]))
    return pairs


CORE = rank_pairs(lambda z, y, c: (z, y, 1 - c))
SIDE = rank_pairs(lambda z, y, c: (z, 1 - y, c))
MID_SIDE = rank_pairs(lambda z, y, c: (z, 1 - y, c) if z in (1, 2) else None)
OUTER = rank_pairs(lambda z, y, c: (z ^ 1, y, c))
INNER = rank_pairs(lambda z, y, c: (3 - z, y, c) if z in (1, 2) else None)
END = rank_pairs(lambda z, y, c: (z ^ 1, y, c) if z in (1, 2) else None)
END_SIDE = rank_pairs(lambda z, y, c: (z ^ 1, 1 - y, c) if z in (1, 2) else None)


def hop(x, pairs):
    return lax.ppermute(x, "rep", pairs)


def place():
    rank = lax.axis_index("rep")
    return rank // 4, (rank // 2) % 2, rank % 2


def slot_kernel(plane_of, dests, rels, owner_ref, *refs):
    lists, refs = refs[:dests], refs[dests:]
    spans, refs = refs[: len(rels)], refs[len(rels) :]
    outs, sems = refs[:dests], refs[dests]
    z, y, c = place()
    copies = []
    for t in range(dests):
        for d in range(2):
            at = [jnp.int32(0)] * len(rels)
            for j in range(LIST):
                block = lists[t][d, j]
                owner = owner_ref[block // SPAN_BLK]
                for k, rel in enumerate(rels):
                    rank = plane_of(z) * 4 + y * 2 + (1 - c if rel else c)
                    at[k] = jnp.where(owner == rank, block % SPAN_BLK, at[k])
            for k, source in enumerate(spans):
                spot = d * len(rels) + k
                copy = pltpu.make_async_copy(
                    source.at[at[k]], outs[t].at[spot], sems.at[t * 2 * len(rels) + spot]
                )
                copy.start()
                copies.append(copy)
    for copy in copies:
        copy.wait()


def slots(plane_of, owner, lists, spans, rels):
    dests = len(lists)
    count = 2 * len(rels)
    shape = jax.ShapeDtypeStruct((count, BLK, 2 * HALF_KV), jnp.bfloat16)
    size = dests * count * BLK * 2 * HALF_KV * 2
    return pl.pallas_call(
        functools.partial(slot_kernel, plane_of, dests, rels),
        out_shape=[shape] * dests,
        in_specs=[SMEM] * (1 + dests) + [ANY] * len(rels),
        out_specs=[VMEM] * dests,
        scratch_shapes=[pltpu.SemaphoreType.DMA((count * dests,))],
        cost_estimate=pl.CostEstimate(flops=0, bytes_accessed=2 * size, transcendentals=0),
        compiler_params=pltpu.CompilerParams(vmem_limit_bytes=8 << 20),
    )(owner, *lists, *[spans[rel].reshape(SPAN_BLK, BLK, 2 * HALF_KV) for rel in rels])


def softmax_part(count, odd, prompt, kv_of, prompt_kv, query, s_ref, p_ref, state_in, state_out, out):
    pieces = count + (1 if prompt else 0)
    row = lax.broadcasted_iota(jnp.int32, (BLK, BLK), 0)
    col = lax.broadcasted_iota(jnp.int32, (BLK, BLK), 1)
    for j in range(pieces):
        keys = prompt_kv(0) if j == count else kv_of(j, 0)
        s_ref[:, j * BLK : (j + 1) * BLK] = lax.dot_general(
            query, keys, (((1,), (1,)), ((), ())), preferred_element_type=jnp.float32
        )
    limits = jnp.where(col < jnp.where(odd, 0, BLK), 0.0, -jnp.inf) if count else None
    scales, tops, totals = [], [], []
    for h in range(GROUP):
        rows = slice(h * BLK, (h + 1) * BLK)

        def score(j):
            part = s_ref[rows, j * BLK : (j + 1) * BLK]
            if j == count:
                return jnp.where(col <= row, part, -jnp.inf)
            if j == count - 1:
                return part + limits
            return part

        top = score(0)
        for j in range(1, pieces):
            top = jnp.maximum(top, score(j))
        top = jnp.max(top, axis=1, keepdims=True)
        if state_in is not None:
            before = state_in[1][:, h : h + 1]
            top = jnp.maximum(top, before)
            scale = jnp.exp2((before - top) * SCALE2)
            scales.append(scale)
        total = None
        for j in range(pieces):
            weight = jnp.exp2((score(j) - top) * SCALE2)
            total = weight if total is None else total + weight
            p_ref[rows, j * BLK : (j + 1) * BLK] = weight.astype(jnp.bfloat16)
        total = jnp.sum(total, axis=1, keepdims=True)
        if state_in is not None:
            total = total + scale * state_in[1][:, GROUP + h : GROUP + h + 1]
        tops.append(top)
        totals.append(total)
    vals = [prompt_kv(1) if j == count else kv_of(j, 1) for j in range(pieces)]
    mixed = lax.dot_general(
        p_ref[:, : pieces * BLK],
        jnp.concatenate(vals, axis=0) if pieces > 1 else vals[0],
        (((1,), (0,)), ((), ())),
        preferred_element_type=jnp.float32,
    )
    stats = jnp.zeros((BLK, BLK), jnp.float32)
    for h in range(GROUP):
        rows = slice(h * BLK, (h + 1) * BLK)
        value = mixed[rows]
        if state_in is not None:
            value = value + scales[h] * state_in[0][rows]
        if out is not None:
            out(h, (value / totals[h]).astype(jnp.bfloat16))
        else:
            state_out[0][rows] = value
            stats = jnp.where(col == h, tops[h], stats)
            stats = jnp.where(col == GROUP + h, totals[h], stats)
    if out is None:
        state_out[1][...] = stats


def attend_kernel(levels, first, final, owner_ref, list_ref, *refs):
    refs = list(refs)
    if first:
        q_ref, pair_q_ref, kp_ref, vp_ref, pair_kv_ref = refs[:5]
        refs = refs[5:]
    else:
        stacked_ref, acc_ref, stats_ref = refs[:3]
        refs = refs[3:]
    table = source_table(levels)
    sources, refs = refs[: len(table)], refs[len(table) :]
    if first:
        stacked_ref = refs.pop(0)
    if final:
        out_ref = refs.pop(0)
    else:
        acc_out, stats_out = refs.pop(0), refs.pop(0)
    held, s_ref, p_ref, count_ref, sems = refs
    room = 4 * len(levels)
    z, y, c = place()
    near = z ^ 1
    mid = jnp.logical_or(z == 1, z == 2)
    inner = jnp.where(mid, 3 - z, 3 - near)
    for d in range(2):

        def fetch(j, count, d=d):
            block = list_ref[d, j]
            owner = owner_ref[block // SPAN_BLK]
            oz, oy, oc = owner // 4, (owner // 2) % 2, owner % 2
            rel = (oc != c).astype(jnp.int32)
            level = jnp.where(oz == z, 0, jnp.where(oz == near, 1, jnp.where(oz == inner, 2, 3)))
            own_column = oy == y
            whole = jnp.logical_and(own_column, jnp.logical_or(level < 2, mid))
            spot_whole = block % SPAN_BLK
            listed = functools.reduce(jnp.logical_or, [level == one for one in levels])
            for (at_level, form, at_rel), source in zip(table, sources):
                if form == "whole":
                    match = jnp.logical_and(whole, rel == at_rel)
                    spot = spot_whole
                elif form == "side":
                    match = jnp.logical_and(~own_column, jnp.logical_or(level < 2, mid))
                    spot = d * 2 + rel
                else:
                    match = jnp.logical_and(
                        ~mid, own_column if form == "end" else ~own_column
                    )
                    match = jnp.logical_and(match, rel == at_rel)
                    spot = d
                match = jnp.logical_and(match, level == at_level)

                @pl.when(match)
                def _(source=source, spot=spot):
                    pltpu.make_async_copy(
                        source.at[spot], held.at[d, count], sems.at[d, count]
                    ).start()

            return count + listed.astype(jnp.int32)

        count_ref[d] = lax.fori_loop(0, LIST, fetch, jnp.int32(0))

    if first:
        for g in range(HALF_HEADS):
            for h in range(GROUP):
                at = (g * GROUP + h) * HEAD_SIZE
                start = pl.multiple_of(c * HALF_Q + at, HEAD_SIZE)
                rows = slice(h * BLK, (h + 1) * BLK)
                stacked_ref[g, rows] = q_ref[:, pl.ds(start, HEAD_SIZE)]
                stacked_ref[HALF_HEADS + g, rows] = pair_q_ref[:, at : at + HEAD_SIZE]
        off = pl.multiple_of(c * HALF_KV, HALF_KV)
        held[0, room, :, :HALF_KV] = kp_ref[:, pl.ds(off, HALF_KV)]
        held[0, room, :, HALF_KV:] = vp_ref[:, pl.ds(off, HALF_KV)]
        held[1, room] = pair_kv_ref[...]

    def part(i, carry):
        d, g = i // HALF_HEADS, i % HALF_HEADS
        count = count_ref[d]

        @pl.when(g == 0)
        def _():
            def arrive(j, carry):
                pltpu.make_async_copy(sources[0].at[0], held.at[d, j], sems.at[d, j]).wait()
                return carry

            lax.fori_loop(0, count, arrive, 0)

            @pl.when(count % 2 == 1)
            def _():
                held[d, count] = jnp.zeros((BLK, 2 * HALF_KV), jnp.bfloat16)

        def kv_of(j, which):
            at = pl.multiple_of(which * HALF_KV + g * HEAD_SIZE, HEAD_SIZE)
            return held[d, j, :, pl.ds(at, HEAD_SIZE)]

        out = None
        if final:

            def out(h, value):
                at = pl.multiple_of((g * GROUP + h) * HEAD_SIZE, HEAD_SIZE)
                out_ref[d, :, pl.ds(at, HEAD_SIZE)] = value

        for even in range(0, room + 1, 2):

            @pl.when((count + 1) // 2 * 2 == even)
            def _(even=even):
                if even == 0 and not first:
                    if final:
                        for h in range(GROUP):
                            value = acc_ref[i, h * BLK : (h + 1) * BLK, :]
                            total = stats_ref[i, :, GROUP + h : GROUP + h + 1]
                            out(h, (value / total).astype(jnp.bfloat16))
                    else:
                        acc_out[i] = acc_ref[i]
                        stats_out[i] = stats_ref[i]
                    return
                softmax_part(
                    even,
                    count % 2 == 1,
                    first,
                    kv_of,
                    lambda which: kv_of(room, which),
                    stacked_ref[i],
                    s_ref,
                    p_ref,
                    None if first else (acc_ref.at[i], stats_ref.at[i]),
                    None if final else (acc_out.at[i], stats_out.at[i]),
                    out,
                )

        return carry

    lax.fori_loop(0, 2 * HALF_HEADS, part, 0)


def source_table(levels):
    table = []
    for level in levels:
        table += [(level, "whole", 0), (level, "whole", 1), (level, "side", None)]
        if level > 1:
            table += [(level, form, rel) for form in ("end", "end_side") for rel in range(2)]
    return table


def attend(levels, first, final, owner, lists, operands, sources):
    parts = 2 * HALF_HEADS
    room = 4 * len(levels)
    pieces = room + (1 if first else 0)
    rows = GROUP * BLK
    stacked = jax.ShapeDtypeStruct((parts, rows, HEAD_SIZE), jnp.bfloat16)
    acc = jax.ShapeDtypeStruct((parts, rows, HEAD_SIZE), jnp.float32)
    stats = jax.ShapeDtypeStruct((parts, BLK, BLK), jnp.float32)
    outs = [stacked] if first else []
    outs += [jax.ShapeDtypeStruct((2, BLK, HALF_Q), jnp.bfloat16)] if final else [acc, stats]
    used = sources_of(levels, sources)
    keys = (pieces + 1) // 2 * BLK
    return pl.pallas_call(
        functools.partial(attend_kernel, levels, first, final),
        out_shape=outs,
        in_specs=[SMEM] * 2 + [VMEM] * len(operands) + [ANY] * len(used),
        out_specs=[VMEM] * len(outs),
        scratch_shapes=[
            pltpu.VMEM((2, room + 1, BLK, 2 * HALF_KV), jnp.bfloat16),
            pltpu.VMEM((rows, pieces * BLK), jnp.float32),
            pltpu.VMEM((rows, pieces * BLK), jnp.bfloat16),
            pltpu.SMEM((2,), jnp.int32),
            pltpu.SemaphoreType.DMA((2, room)),
        ],
        cost_estimate=pl.CostEstimate(
            flops=4 * QUERY_HEADS * BLK * keys * HEAD_SIZE,
            bytes_accessed=4 << 20,
            transcendentals=QUERY_HEADS * BLK * keys,
        ),
        compiler_params=pltpu.CompilerParams(vmem_limit_bytes=30 << 20),
    )(owner, lists, *operands, *used)


def sources_of(levels, sources):
    return [sources[key].reshape(-1, BLK, 2 * HALF_KV) for key in source_table(levels)]


def line_device(
    queries,
    prompt_keys,
    prompt_value_rows,
    document_keys,
    document_values,
    span_owner,
    block_list,
    prompt_length,
):
    first = lax.axis_index("rep") % 2 == 0

    def half(x, mine):
        width = x.shape[1] // 2
        return jnp.where(first == mine, x[:, :width], x[:, width:])

    def paired(keys, values, mine):
        return jnp.concatenate([half(keys, mine), half(values, mine)], axis=1)

    own = [paired(document_keys, document_values, True)]
    own.append(hop(paired(document_keys, document_values, False), CORE))
    outer = [hop(x, OUTER) for x in own]
    inner = [hop(x, INNER) for x in own]
    far = [hop(x, INNER) for x in outer]

    lists = jnp.concatenate([block_list, hop(block_list, CORE)], axis=0)
    side_lists = hop(lists, SIDE)
    end_lists = hop(jnp.concatenate([lists, side_lists], axis=0), OUTER)
    pair_q = hop(half(queries, False), CORE)
    pair_kv = hop(paired(prompt_keys, prompt_value_rows, False), CORE)

    planes = [lambda z: z, lambda z: z ^ 1, lambda z: 3 - z, lambda z: (3 - z) ^ 1]
    sources = {}
    for level, spans in enumerate((own, outer, inner, far)):
        for rel in range(2):
            sources[level, "whole", rel] = spans[rel]
        (side,) = slots(planes[level], span_owner, [side_lists], spans, (0, 1))
        sources[level, "side", None] = hop(side, SIDE if level < 2 else MID_SIDE)
        if level > 1:
            for rel in range(2):
                end, end_side = slots(
                    planes[level], span_owner, [end_lists[:2], end_lists[2:]], spans, (rel,)
                )
                sources[level, "end", rel] = hop(end, END)
                sources[level, "end_side", rel] = hop(end_side, END_SIDE)

    operands = [queries, pair_q, prompt_keys, prompt_value_rows, pair_kv]
    stacked, acc, stats = attend((0, 1), True, False, span_owner, lists, operands, sources)
    acc, stats = attend((2,), False, False, span_owner, lists, [stacked, acc, stats], sources)
    (halves,) = attend((3,), False, True, span_owner, lists, [stacked, acc, stats], sources)
    mine, theirs = halves[0], hop(halves[1], CORE)
    joined = jnp.where(
        first,
        jnp.concatenate([mine, theirs], axis=1),
        jnp.concatenate([theirs, mine], axis=1),
    )
    live = jnp.arange(BLK, dtype=jnp.int32) < prompt_length[0]
    return jnp.where(live[:, None], joined, jnp.zeros_like(joined))


def probs_of(query_part, key_part, visible):
    scores = jnp.einsum(
        "thd,kd->htk", query_part, key_part, preferred_element_type=jnp.float32
    ) * query_part.shape[-1] ** (-0.5)
    scores = jnp.where(visible[None], scores, -jnp.inf)
    largest = jnp.max(scores, axis=-1, keepdims=True)
    weights = jnp.exp(scores - largest)
    return (weights / jnp.sum(weights, axis=-1, keepdims=True)).astype(jnp.bfloat16)


def per_device(
    queries,
    prompt_keys,
    prompt_value_rows,
    document_keys,
    document_values,
    span_owner,
    block_list,
    prompt_length,
):
    group_width = QUERY_HEADS // KEY_VALUE_HEADS
    count = lax.axis_size("rep")
    list_len = block_list.shape[1]
    all_ranks = jnp.arange(count, dtype=jnp.int32)
    my_list = block_list[0]
    list_span = my_list // SPAN_BLK
    owners = jnp.sum(
        jnp.where(list_span[:, None] == all_ranks[None, :], span_owner[None, :], 0), axis=1
    )
    matches = owners[None, :] == all_ranks[:, None]
    request = jnp.sum(jnp.where(matches, (my_list % SPAN_BLK + 1)[None, :], 0), axis=1) - 1
    arrived = lax.all_to_all(request, "rep", split_axis=0, concat_axis=0, tiled=True)
    wanted = arrived >= 0
    inner_block = jnp.maximum(arrived, 0)

    def outgoing(source):
        blocks = source.reshape(SPAN_BLK, BLK, source.shape[1])
        picked = jnp.take(blocks, inner_block, axis=0)
        return jnp.where(wanted[:, None, None], picked, jnp.zeros_like(picked))

    def listed(received):
        return jnp.take(received, owners, axis=0).reshape(list_len * BLK, received.shape[2])

    send_keys = outgoing(document_keys)
    send_values = outgoing(document_values)
    doc_visible = jnp.ones((BLK, list_len * BLK), dtype=bool)
    got_keys, got_values = (
        lax.all_to_all(send_keys, "rep", split_axis=0, concat_axis=0, tiled=True),
        lax.all_to_all(send_values, "rep", split_axis=0, concat_axis=0, tiled=True),
    )
    query_block = 0
    seen = (query_block + 1) * BLK
    key_rows = jnp.concatenate([listed(got_keys), prompt_keys], axis=0)
    slots = jnp.arange(seen, dtype=jnp.int32)
    positions = query_block * BLK + jnp.arange(BLK, dtype=jnp.int32)
    visible = jnp.concatenate([doc_visible, slots[None, :] <= positions[:, None]], axis=1)
    row_probs = []
    for all_head_cluster in range(KEY_VALUE_HEADS):
        cols = slice(
            all_head_cluster * group_width * HEAD_SIZE,
            (all_head_cluster + 1) * group_width * HEAD_SIZE,
        )
        query_part = queries[query_block * BLK : seen, cols].reshape(BLK, group_width, HEAD_SIZE)
        row_probs.append(
            probs_of(
                query_part,
                key_rows[:, all_head_cluster * HEAD_SIZE : (all_head_cluster + 1) * HEAD_SIZE],
                visible,
            )
        )
    table = [row_probs]
    doc_value_rows = listed(got_values)
    live_rows = prompt_length[0]
    query_block = 0
    value_rows = jnp.concatenate([doc_value_rows, prompt_value_rows], axis=0)
    pieces = []
    for head_cluster in range(KEY_VALUE_HEADS):
        mixed = jnp.einsum(
            "htk,kd->thd",
            table[query_block][head_cluster],
            value_rows[:, head_cluster * HEAD_SIZE : (head_cluster + 1) * HEAD_SIZE],
            preferred_element_type=jnp.float32,
        )
        pieces.append(mixed.reshape(BLK, group_width * HEAD_SIZE))
    joined = jnp.concatenate(pieces, axis=1).astype(jnp.bfloat16)
    positions = query_block * BLK + jnp.arange(BLK, dtype=jnp.int32)
    outputs = jnp.where((positions < live_rows)[:, None], joined, jnp.zeros_like(joined))
    return outputs


def solution(mesh):
    body = line_device if mesh.shape["rep"] == 16 else per_device
    return jax.shard_map(
        body,
        mesh=mesh,
        in_specs=(
            P(("group", "rep"), None),
            P(("group", "rep"), None),
            P(("group", "rep"), None),
            P(("group", "rep"), None),
            P(("group", "rep"), None),
            P("group"),
            P(("group", "rep"), None),
            P(("group", "rep")),
        ),
        out_specs=P(("group", "rep"), None),
        check_vma=False,
    )
```

```python
import functools
import math

import jax
import jax.numpy as jnp
from jax import lax
from jax.experimental import pallas as pl
from jax.experimental.pallas import tpu as pltpu
from jax.sharding import PartitionSpec as P

QUERY_HEADS = 32
KEY_VALUE_HEADS = 4
HEAD_SIZE = 128
BLK = 128
SPAN_BLK = 4
LIST = 8
GROUP = QUERY_HEADS // KEY_VALUE_HEADS
HALF_HEADS = KEY_VALUE_HEADS // 2
HALF_KV = HALF_HEADS * HEAD_SIZE
HALF_Q = HALF_HEADS * GROUP * HEAD_SIZE
SCALE2 = math.log2(math.e) / math.sqrt(HEAD_SIZE)


SMEM = pl.BlockSpec(memory_space=pltpu.SMEM)
VMEM = pl.BlockSpec(memory_space=pltpu.VMEM)
ANY = pl.BlockSpec(memory_space=pl.ANY)


def rank_pairs(move):
    pairs = []
    for z in range(4):
        for y in range(2):
            for c in range(2):
                to = move(z, y, c)
                if to is not None:
                    pairs.append((z * 4 + y * 2 + c, to[0] * 4 + to[1] * 2 + to[2]))
    return pairs


CORE = rank_pairs(lambda z, y, c: (z, y, 1 - c))
SIDE = rank_pairs(lambda z, y, c: (z, 1 - y, c))
MID_SIDE = rank_pairs(lambda z, y, c: (z, 1 - y, c) if z in (1, 2) else None)
OUTER = rank_pairs(lambda z, y, c: (z ^ 1, y, c))
INNER = rank_pairs(lambda z, y, c: (3 - z, y, c) if z in (1, 2) else None)
END = rank_pairs(lambda z, y, c: (z ^ 1, y, c) if z in (1, 2) else None)
END_SIDE = rank_pairs(lambda z, y, c: (z ^ 1, 1 - y, c) if z in (1, 2) else None)


def hop(x, pairs):
    return lax.ppermute(x, "rep", pairs)


def place():
    rank = lax.axis_index("rep")
    return rank // 4, (rank // 2) % 2, rank % 2


def slot_kernel(plane_of, dests, rels, owner_ref, *refs):
    lists, refs = refs[:dests], refs[dests:]
    spans, refs = refs[: len(rels)], refs[len(rels) + 1 :]
    outs, sems = refs[:dests], refs[dests]
    z, y, c = place()
    copies = []
    for t in range(dests):
        for d in range(2):
            at = [jnp.int32(0)] * len(rels)
            for j in range(LIST):
                block = lists[t][d, j]
                owner = owner_ref[block // SPAN_BLK]
                for k, rel in enumerate(rels):
                    rank = plane_of(z) * 4 + y * 2 + (1 - c if rel else c)
                    at[k] = jnp.where(owner == rank, block % SPAN_BLK, at[k])
            for k, source in enumerate(spans):
                spot = d * len(rels) + k
                copy = pltpu.make_async_copy(
                    source.at[at[k]], outs[t].at[spot], sems.at[t * 2 * len(rels) + spot]
                )
                copy.start()
                copies.append(copy)
    for copy in copies:
        copy.wait()


def slots(plane_of, owner, lists, spans, rels, after):
    dests = len(lists)
    count = 2 * len(rels)
    shape = jax.ShapeDtypeStruct((count, BLK, 2 * HALF_KV), jnp.bfloat16)
    size = dests * count * BLK * 2 * HALF_KV * 2
    return pl.pallas_call(
        functools.partial(slot_kernel, plane_of, dests, rels),
        out_shape=[shape] * dests,
        in_specs=[SMEM] * (1 + dests) + [ANY] * (len(rels) + 1),
        out_specs=[VMEM] * dests,
        scratch_shapes=[pltpu.SemaphoreType.DMA((count * dests,))],
        cost_estimate=pl.CostEstimate(flops=0, bytes_accessed=2 * size, transcendentals=0),
        compiler_params=pltpu.CompilerParams(vmem_limit_bytes=8 << 20),
    )(owner, *lists, *[spans[rel].reshape(SPAN_BLK, BLK, 2 * HALF_KV) for rel in rels], after)


def softmax_part(blocks, odd, prompt, held_of, query, s_ref, p_ref, state_in, state_out, out):
    pieces = blocks + (1 if prompt else 0)
    row = lax.broadcasted_iota(jnp.int32, (BLK, BLK), 0)
    col = lax.broadcasted_iota(jnp.int32, (BLK, BLK), 1)
    width = pieces * BLK
    s_ref[:, :width] = lax.dot_general(
        query, held_of(pieces, 0), (((1,), (1,)), ((), ())), preferred_element_type=jnp.float32
    )
    scales, tops, totals = [], [], []
    for h in range(GROUP):
        rows = slice(h * BLK, (h + 1) * BLK)
        parts = []
        for j in range(pieces):
            part = s_ref[rows, j * BLK : (j + 1) * BLK]
            if prompt and j == 0:
                part = jnp.where(col <= row, part, -jnp.inf)
            elif j == pieces - 1:
                part = jnp.where(odd, -jnp.inf, part)
            parts.append(part)
        top = functools.reduce(jnp.maximum, parts)
        top = jnp.max(top, axis=1, keepdims=True)
        if state_in is not None:
            before = state_in[1][:, h : h + 1]
            top = jnp.maximum(top, before)
            scale = jnp.exp2((before - top) * SCALE2)
            scales.append(scale)
        total = None
        for j, part in enumerate(parts):
            weight = jnp.exp2((part - top) * SCALE2)
            total = weight if total is None else total + weight
            p_ref[rows, j * BLK : (j + 1) * BLK] = weight.astype(jnp.bfloat16)
        total = jnp.sum(total, axis=1, keepdims=True)
        if state_in is not None:
            total = total + scale * state_in[1][:, GROUP + h : GROUP + h + 1]
        tops.append(top)
        totals.append(total)
    mixed = lax.dot_general(
        p_ref[:, :width],
        held_of(pieces, 1),
        (((1,), (0,)), ((), ())),
        preferred_element_type=jnp.float32,
    )
    stats = jnp.zeros((BLK, BLK), jnp.float32)
    for h in range(GROUP):
        rows = slice(h * BLK, (h + 1) * BLK)
        value = mixed[rows]
        if state_in is not None:
            value = value + scales[h] * state_in[0][rows]
        if out is not None:
            out(h, (value * (1.0 / totals[h])).astype(jnp.bfloat16))
        else:
            state_out[0][rows] = value
            stats = jnp.where(col == h, tops[h], stats)
            stats = jnp.where(col == GROUP + h, totals[h], stats)
    if out is None:
        state_out[1][...] = stats


def attend_kernel(levels, first, final, owner_ref, list_ref, *refs):
    refs = list(refs)
    if first:
        q_ref, pair_q_ref, kp_ref, vp_ref, pair_kv_ref = refs[:5]
        refs = refs[5:]
    else:
        stacked_ref, acc_ref, stats_ref = refs[:3]
        refs = refs[3:]
    table = source_table(levels)
    sources, refs = refs[: len(table)], refs[len(table) + 1 :]
    if first:
        stacked_ref = refs.pop(0)
    if final:
        out_ref = refs.pop(0)
    else:
        acc_out, stats_out = refs.pop(0), refs.pop(0)
    held, s_ref, p_ref, count_ref, sems = refs
    room = min(4 * len(levels), LIST)
    base = 1 if first else 0
    z, y, c = place()
    near = z ^ 1
    mid = jnp.logical_or(z == 1, z == 2)
    inner = jnp.where(mid, 3 - z, 3 - near)
    for d in range(2):

        def fetch(j, count, d=d):
            block = list_ref[d, j]
            owner = owner_ref[block // SPAN_BLK]
            oz, oy, oc = owner // 4, (owner // 2) % 2, owner % 2
            rel = (oc != c).astype(jnp.int32)
            level = jnp.where(oz == z, 0, jnp.where(oz == near, 1, jnp.where(oz == inner, 2, 3)))
            own_column = oy == y
            whole = jnp.logical_and(own_column, jnp.logical_or(level < 2, mid))
            spot_whole = block % SPAN_BLK
            listed = functools.reduce(jnp.logical_or, [level == one for one in levels])
            for (at_level, form, at_rel), source in zip(table, sources):
                if form == "whole":
                    match = jnp.logical_and(whole, rel == at_rel)
                    spot = spot_whole
                elif form == "side":
                    match = jnp.logical_and(~own_column, jnp.logical_or(level < 2, mid))
                    spot = d * 2 + rel
                else:
                    match = jnp.logical_and(
                        ~mid, own_column if form == "end" else ~own_column
                    )
                    match = jnp.logical_and(match, rel == at_rel)
                    spot = d
                match = jnp.logical_and(match, level == at_level)

                @pl.when(match)
                def _(source=source, spot=spot):
                    pltpu.make_async_copy(
                        source.at[spot], held.at[d, base + count], sems.at[d, count]
                    ).start()

            return count + listed.astype(jnp.int32)

        count_ref[d] = lax.fori_loop(0, LIST, fetch, jnp.int32(0))

    if first:
        for g in range(HALF_HEADS):
            for h in range(GROUP):
                at = (g * GROUP + h) * HEAD_SIZE
                start = pl.multiple_of(c * HALF_Q + at, HEAD_SIZE)
                rows = slice(h * BLK, (h + 1) * BLK)
                stacked_ref[g, rows] = q_ref[:, pl.ds(start, HEAD_SIZE)]
                stacked_ref[HALF_HEADS + g, rows] = pair_q_ref[:, at : at + HEAD_SIZE]
        off = pl.multiple_of(c * HALF_KV, HALF_KV)
        held[0, 0, :, :HALF_KV] = kp_ref[:, pl.ds(off, HALF_KV)]
        held[0, 0, :, HALF_KV:] = vp_ref[:, pl.ds(off, HALF_KV)]
        held[1, 0] = pair_kv_ref[...]

    def part(i, carry):
        d, g = i // HALF_HEADS, i % HALF_HEADS
        count = count_ref[d]

        @pl.when(g == 0)
        def _():
            def arrive(j, carry):
                pltpu.make_async_copy(sources[0].at[0], held.at[d, base + j], sems.at[d, j]).wait()
                return carry

            lax.fori_loop(0, count, arrive, 0)

            @pl.when(count % 2 == 1)
            def _():
                held[d, base + count] = jnp.zeros((BLK, 2 * HALF_KV), jnp.bfloat16)

        def held_of(pieces, which):
            at = pl.multiple_of(which * HALF_KV + g * HEAD_SIZE, HEAD_SIZE)
            return held[d, :pieces, :, pl.ds(at, HEAD_SIZE)].reshape(pieces * BLK, HEAD_SIZE)

        out = None
        if final:

            def out(h, value):
                at = pl.multiple_of((g * GROUP + h) * HEAD_SIZE, HEAD_SIZE)
                out_ref[d, :, pl.ds(at, HEAD_SIZE)] = value

        for even in range(0, room + 1, 2):

            @pl.when((count + 1) // 2 * 2 == even)
            def _(even=even):
                if even == 0 and not first:
                    if final:
                        for h in range(GROUP):
                            value = acc_ref[i, h * BLK : (h + 1) * BLK, :]
                            total = stats_ref[i, :, GROUP + h : GROUP + h + 1]
                            out(h, (value * (1.0 / total)).astype(jnp.bfloat16))
                    else:
                        acc_out[i] = acc_ref[i]
                        stats_out[i] = stats_ref[i]
                    return
                softmax_part(
                    even,
                    count % 2 == 1,
                    first,
                    held_of,
                    stacked_ref[i],
                    s_ref,
                    p_ref,
                    None if first else (acc_ref.at[i], stats_ref.at[i]),
                    None if final else (acc_out.at[i], stats_out.at[i]),
                    out,
                )

        return carry

    lax.fori_loop(0, 2 * HALF_HEADS, part, 0)


def source_table(levels):
    table = []
    for level in levels:
        table += [(level, "whole", 0), (level, "whole", 1), (level, "side", None)]
        if level > 1:
            table += [(level, form, rel) for form in ("end", "end_side") for rel in range(2)]
    return table


def attend(levels, first, final, owner, lists, operands, sources, after):
    parts = 2 * HALF_HEADS
    room = min(4 * len(levels), LIST)
    pieces = room + (1 if first else 0)
    rows = GROUP * BLK
    stacked = jax.ShapeDtypeStruct((parts, rows, HEAD_SIZE), jnp.bfloat16)
    acc = jax.ShapeDtypeStruct((parts, rows, HEAD_SIZE), jnp.float32)
    stats = jax.ShapeDtypeStruct((parts, BLK, BLK), jnp.float32)
    outs = [stacked] if first else []
    outs += [jax.ShapeDtypeStruct((2, BLK, HALF_Q), jnp.bfloat16)] if final else [acc, stats]
    used = sources_of(levels, sources)
    keys = (pieces + 1) // 2 * BLK
    return pl.pallas_call(
        functools.partial(attend_kernel, levels, first, final),
        out_shape=outs,
        in_specs=[SMEM] * 2 + [VMEM] * len(operands) + [ANY] * (len(used) + 1),
        out_specs=[VMEM] * len(outs),
        scratch_shapes=[
            pltpu.VMEM((2, room + 1, BLK, 2 * HALF_KV), jnp.bfloat16),
            pltpu.VMEM((rows, pieces * BLK), jnp.float32),
            pltpu.VMEM((rows, pieces * BLK), jnp.bfloat16),
            pltpu.SMEM((2,), jnp.int32),
            pltpu.SemaphoreType.DMA((2, room)),
        ],
        cost_estimate=pl.CostEstimate(
            flops=4 * QUERY_HEADS * BLK * keys * HEAD_SIZE,
            bytes_accessed=4 << 20,
            transcendentals=QUERY_HEADS * BLK * keys,
        ),
        compiler_params=pltpu.CompilerParams(vmem_limit_bytes=30 << 20),
    )(owner, lists, *operands, *used, after)


def sources_of(levels, sources):
    return [sources[key].reshape(-1, BLK, 2 * HALF_KV) for key in source_table(levels)]


def line_device(
    queries,
    prompt_keys,
    prompt_value_rows,
    document_keys,
    document_values,
    span_owner,
    block_list,
    prompt_length,
):
    first = lax.axis_index("rep") % 2 == 0

    def half(x, mine):
        width = x.shape[1] // 2
        return jnp.where(first == mine, x[:, :width], x[:, width:])

    def paired(keys, values, mine):
        return jnp.concatenate([half(keys, mine), half(values, mine)], axis=1)

    own = [paired(document_keys, document_values, True)]
    own.append(hop(paired(document_keys, document_values, False), CORE))
    outer = [hop(own[rel], OUTER) for rel in range(2)]
    inner = [hop(own[rel], INNER) for rel in range(2)]
    far = [hop(outer[rel], INNER) for rel in range(2)]

    ahead = hop(block_list, OUTER)
    both = jnp.concatenate([block_list, ahead], axis=0)
    across = hop(both, CORE)
    four = jnp.concatenate([both, across], axis=0)
    beside = hop(four, SIDE)

    def chip_lists(four, at):
        return jnp.concatenate([four[at : at + 1], four[at + 2 : at + 3]], axis=0)

    lists, side_lists = chip_lists(four, 0), chip_lists(beside, 0)
    near_lists = [chip_lists(four, 1), chip_lists(beside, 1)]
    pair_q = hop(half(queries, False), CORE)
    pair_kv = hop(paired(prompt_keys, prompt_value_rows, False), CORE)

    planes = [lambda z: z, lambda z: z ^ 1, lambda z: 3 - z, lambda z: (3 - z) ^ 1]
    spans = (own, outer, inner, far)
    sources = {(level, "whole", rel): spans[level][rel] for level in range(4) for rel in range(2)}

    def send_side(level, after):
        (side,) = slots(planes[level], span_owner, [side_lists], spans[level], (0, 1), after)
        sources[level, "side", None] = hop(side, SIDE if level < 2 else MID_SIDE)
        return side

    def send_end(level, rel, after):
        end, end_side = slots(planes[level], span_owner, near_lists, spans[level], (rel,), after)
        sources[level, "end", rel] = hop(end, END)
        sources[level, "end_side", rel] = hop(end_side, END_SIDE)
        return end

    last = send_side(0, own[0])
    last = send_end(2, 0, last)
    last = send_side(1, last)
    last = send_end(2, 1, last)
    last = send_side(2, last)
    last = send_end(3, 0, last)
    last = send_end(3, 1, last)
    last = send_side(3, last)
    operands = [queries, pair_q, prompt_keys, prompt_value_rows, pair_kv]
    operands = attend((0, 1, 2), True, False, span_owner, lists, operands, sources, last)
    (halves,) = attend((3,), False, True, span_owner, lists, operands, sources, last)
    mine, theirs = halves[0], hop(halves[1], CORE)
    joined = jnp.where(
        first,
        jnp.concatenate([mine, theirs], axis=1),
        jnp.concatenate([theirs, mine], axis=1),
    )
    live = jnp.arange(BLK, dtype=jnp.int32) < prompt_length[0]
    return jnp.where(live[:, None], joined, jnp.zeros_like(joined))


def probs_of(query_part, key_part, visible):
    scores = jnp.einsum(
        "thd,kd->htk", query_part, key_part, preferred_element_type=jnp.float32
    ) * query_part.shape[-1] ** (-0.5)
    scores = jnp.where(visible[None], scores, -jnp.inf)
    largest = jnp.max(scores, axis=-1, keepdims=True)
    weights = jnp.exp(scores - largest)
    return (weights / jnp.sum(weights, axis=-1, keepdims=True)).astype(jnp.bfloat16)


def per_device(
    queries,
    prompt_keys,
    prompt_value_rows,
    document_keys,
    document_values,
    span_owner,
    block_list,
    prompt_length,
):
    group_width = QUERY_HEADS // KEY_VALUE_HEADS
    count = lax.axis_size("rep")
    list_len = block_list.shape[1]
    all_ranks = jnp.arange(count, dtype=jnp.int32)
    my_list = block_list[0]
    list_span = my_list // SPAN_BLK
    owners = jnp.sum(
        jnp.where(list_span[:, None] == all_ranks[None, :], span_owner[None, :], 0), axis=1
    )
    matches = owners[None, :] == all_ranks[:, None]
    request = jnp.sum(jnp.where(matches, (my_list % SPAN_BLK + 1)[None, :], 0), axis=1) - 1
    arrived = lax.all_to_all(request, "rep", split_axis=0, concat_axis=0, tiled=True)
    wanted = arrived >= 0
    inner_block = jnp.maximum(arrived, 0)

    def outgoing(source):
        blocks = source.reshape(SPAN_BLK, BLK, source.shape[1])
        picked = jnp.take(blocks, inner_block, axis=0)
        return jnp.where(wanted[:, None, None], picked, jnp.zeros_like(picked))

    def listed(received):
        return jnp.take(received, owners, axis=0).reshape(list_len * BLK, received.shape[2])

    send_keys = outgoing(document_keys)
    send_values = outgoing(document_values)
    doc_visible = jnp.ones((BLK, list_len * BLK), dtype=bool)
    got_keys, got_values = (
        lax.all_to_all(send_keys, "rep", split_axis=0, concat_axis=0, tiled=True),
        lax.all_to_all(send_values, "rep", split_axis=0, concat_axis=0, tiled=True),
    )
    query_block = 0
    seen = (query_block + 1) * BLK
    key_rows = jnp.concatenate([listed(got_keys), prompt_keys], axis=0)
    slots = jnp.arange(seen, dtype=jnp.int32)
    positions = query_block * BLK + jnp.arange(BLK, dtype=jnp.int32)
    visible = jnp.concatenate([doc_visible, slots[None, :] <= positions[:, None]], axis=1)
    row_probs = []
    for all_head_cluster in range(KEY_VALUE_HEADS):
        cols = slice(
            all_head_cluster * group_width * HEAD_SIZE,
            (all_head_cluster + 1) * group_width * HEAD_SIZE,
        )
        query_part = queries[query_block * BLK : seen, cols].reshape(BLK, group_width, HEAD_SIZE)
        row_probs.append(
            probs_of(
                query_part,
                key_rows[:, all_head_cluster * HEAD_SIZE : (all_head_cluster + 1) * HEAD_SIZE],
                visible,
            )
        )
    table = [row_probs]
    doc_value_rows = listed(got_values)
    live_rows = prompt_length[0]
    query_block = 0
    value_rows = jnp.concatenate([doc_value_rows, prompt_value_rows], axis=0)
    pieces = []
    for head_cluster in range(KEY_VALUE_HEADS):
        mixed = jnp.einsum(
            "htk,kd->thd",
            table[query_block][head_cluster],
            value_rows[:, head_cluster * HEAD_SIZE : (head_cluster + 1) * HEAD_SIZE],
            preferred_element_type=jnp.float32,
        )
        pieces.append(mixed.reshape(BLK, group_width * HEAD_SIZE))
    joined = jnp.concatenate(pieces, axis=1).astype(jnp.bfloat16)
    positions = query_block * BLK + jnp.arange(BLK, dtype=jnp.int32)
    outputs = jnp.where((positions < live_rows)[:, None], joined, jnp.zeros_like(joined))
    return outputs


def layered(*args):
    return line_device(*args)


def solution(mesh):
    line = mesh.shape["rep"] == 16
    return jax.shard_map(
        layered if line else per_device,
        mesh=mesh,
        in_specs=(
            P(("group", "rep"), None),
            P(("group", "rep"), None),
            P(("group", "rep"), None),
            P(("group", "rep"), None),
            P(("group", "rep"), None),
            P("group"),
            P(("group", "rep"), None),
            P(("group", "rep")),
        ),
        out_specs=P(("group", "rep"), None),
        check_vma=False,
    )
```

```python
import functools
import math

import jax
import jax.numpy as jnp
from jax import lax
from jax.experimental import pallas as pl
from jax.experimental.pallas import tpu as pltpu
from jax.sharding import PartitionSpec as P

QUERY_HEADS = 32
KEY_VALUE_HEADS = 4
HEAD_SIZE = 128
BLK = 128
SPAN_BLK = 4
LIST = 8
GROUP = QUERY_HEADS // KEY_VALUE_HEADS
HALF_HEADS = KEY_VALUE_HEADS // 2
HALF_KV = HALF_HEADS * HEAD_SIZE
HALF_Q = HALF_HEADS * GROUP * HEAD_SIZE
SCALE2 = math.log2(math.e) / math.sqrt(HEAD_SIZE)

GROUPS = (
    (),
    tuple(
        (level, form, rel)
        for level in range(2)
        for form, rel in (("whole", 0), ("whole", 1), ("side", None))
    )
    + ((2, "whole", 0), (2, "whole", 1), (2, "side", None))
    + ((2, "end", 0), (2, "end", 1), (2, "end_side", 0), (2, "end_side", 1)),
    ((3, "whole", 0), (3, "side", 0), (3, "end", 0), (3, "end_side", 0)),
    ((3, "whole", 1), (3, "side", 1), (3, "end", 1), (3, "end_side", 1)),
)
ROOMS = (0, 8, 2, 2)


SMEM = pl.BlockSpec(memory_space=pltpu.SMEM)
VMEM = pl.BlockSpec(memory_space=pltpu.VMEM)
ANY = pl.BlockSpec(memory_space=pl.ANY)


def rank_pairs(move):
    pairs = []
    for z in range(4):
        for y in range(2):
            for c in range(2):
                to = move(z, y, c)
                if to is not None:
                    pairs.append((z * 4 + y * 2 + c, to[0] * 4 + to[1] * 2 + to[2]))
    return pairs


CORE = rank_pairs(lambda z, y, c: (z, y, 1 - c))
SIDE = rank_pairs(lambda z, y, c: (z, 1 - y, c))
MID_SIDE = rank_pairs(lambda z, y, c: (z, 1 - y, c) if z in (1, 2) else None)
OUTER = rank_pairs(lambda z, y, c: (z ^ 1, y, c))
INNER = rank_pairs(lambda z, y, c: (3 - z, y, c) if z in (1, 2) else None)
END = rank_pairs(lambda z, y, c: (z ^ 1, y, c) if z in (1, 2) else None)
END_SIDE = rank_pairs(lambda z, y, c: (z ^ 1, 1 - y, c) if z in (1, 2) else None)


def hop(x, pairs):
    return lax.ppermute(x, "rep", pairs)


def place():
    rank = lax.axis_index("rep")
    return rank // 4, (rank // 2) % 2, rank % 2


def slot_kernel(plane_of, dests, rels, owner_ref, *refs):
    lists, refs = refs[:dests], refs[dests:]
    spans, refs = refs[: len(rels)], refs[len(rels) + 1 :]
    outs, sems = refs[:dests], refs[dests]
    z, y, c = place()
    copies = []
    for t in range(dests):
        for d in range(2):
            at = [jnp.int32(0)] * len(rels)
            for j in range(LIST):
                block = lists[t][d, j]
                owner = owner_ref[block // SPAN_BLK]
                for k, rel in enumerate(rels):
                    rank = plane_of(z) * 4 + y * 2 + (1 - c if rel else c)
                    at[k] = jnp.where(owner == rank, block % SPAN_BLK, at[k])
            for k, source in enumerate(spans):
                spot = d * len(rels) + k
                copy = pltpu.make_async_copy(
                    source.at[at[k]], outs[t].at[spot], sems.at[t * 2 * len(rels) + spot]
                )
                copy.start()
                copies.append(copy)
    for copy in copies:
        copy.wait()


def slots(plane_of, owner, lists, spans, rels, after):
    dests = len(lists)
    count = 2 * len(rels)
    shape = jax.ShapeDtypeStruct((count, BLK, 2 * HALF_KV), jnp.bfloat16)
    size = dests * count * BLK * 2 * HALF_KV * 2
    return pl.pallas_call(
        functools.partial(slot_kernel, plane_of, dests, rels),
        out_shape=[shape] * dests,
        in_specs=[SMEM] * (1 + dests) + [ANY] * (len(rels) + 1),
        out_specs=[VMEM] * dests,
        scratch_shapes=[pltpu.SemaphoreType.DMA((count * dests,))],
        cost_estimate=pl.CostEstimate(flops=0, bytes_accessed=2 * size, transcendentals=0),
        compiler_params=pltpu.CompilerParams(vmem_limit_bytes=8 << 20),
    )(owner, *lists, *[spans[rel].reshape(SPAN_BLK, BLK, 2 * HALF_KV) for rel in rels], after)


def softmax_part(blocks, odd, prompt, held_of, query, s_ref, p_ref, state_in, state_out, out):
    pieces = blocks + (1 if prompt else 0)
    row = lax.broadcasted_iota(jnp.int32, (BLK, BLK), 0)
    col = lax.broadcasted_iota(jnp.int32, (BLK, BLK), 1)
    width = pieces * BLK
    s_ref[:, :width] = lax.dot_general(
        query, held_of(pieces, 0), (((1,), (1,)), ((), ())), preferred_element_type=jnp.float32
    )
    scales, totals = [], []
    for h in range(GROUP):
        rows = slice(h * BLK, (h + 1) * BLK)
        parts = []
        for j in range(pieces):
            part = s_ref[rows, j * BLK : (j + 1) * BLK]
            if prompt and j == 0:
                part = jnp.where(col <= row, part, -jnp.inf)
            elif j == pieces - 1 and odd is not None:
                part = jnp.where(odd, -jnp.inf, part)
            parts.append(part)
        top = functools.reduce(jnp.maximum, parts)
        top = jnp.broadcast_to(jnp.max(top, axis=1, keepdims=True), (BLK, BLK))
        if state_in is not None:
            before = state_in[1][rows]
            top = jnp.maximum(top, before)
            scale = jnp.exp2((before - top) * SCALE2)
            scales.append(scale)
        total = None
        for j, part in enumerate(parts):
            weight = jnp.exp2((part - top) * SCALE2)
            total = weight if total is None else total + weight
            p_ref[rows, j * BLK : (j + 1) * BLK] = weight.astype(jnp.bfloat16)
        total = jnp.broadcast_to(jnp.sum(total, axis=1, keepdims=True), (BLK, BLK))
        if state_in is not None:
            total = total + scale * state_in[2][rows]
        if out is None:
            state_out[1][rows] = top
            state_out[2][rows] = total
        else:
            totals.append(total)
    mixed = lax.dot_general(
        p_ref[:, :width],
        held_of(pieces, 1),
        (((1,), (0,)), ((), ())),
        preferred_element_type=jnp.float32,
    )
    for h in range(GROUP):
        rows = slice(h * BLK, (h + 1) * BLK)
        value = mixed[rows]
        if state_in is not None:
            value = value + scales[h] * state_in[0][rows]
        if out is not None:
            out(h, (value * (1.0 / totals[h])).astype(jnp.bfloat16))
        else:
            state_out[0][rows] = value


def attend_kernel(group, owner_ref, list_ref, *refs):
    first, final = group == 0, group == len(GROUPS) - 1
    refs = list(refs)
    if first:
        q_ref, pair_q_ref, kp_ref, vp_ref, pair_kv_ref = refs[:5]
        refs = refs[5:]
    else:
        stacked_ref, acc_ref, top_ref, total_ref, plan_ref = refs[:5]
        refs = refs[5:]
    table = GROUPS[group]
    sources, refs = refs[: len(table)], refs[len(table) + 1 :]
    if first:
        stacked_ref, plan_ref = refs[:2]
        refs = refs[2:]
    if final:
        out_ref = refs.pop(0)
    else:
        acc_out, top_out, total_out = refs[:3]
        refs = refs[3:]
    held, s_ref, p_ref, sems = refs
    room = ROOMS[group]
    base = 1 if first else 0
    z, y, c = place()
    if first:
        near = z ^ 1
        mid = jnp.logical_or(z == 1, z == 2)
        inner = jnp.where(mid, 3 - z, 3 - near)
        for d in range(2):
            for at in range(len(GROUPS)):
                plan_ref[at, d, 0] = jnp.int32(0)

            def place_block(j, carry, d=d):
                block = list_ref[d, j]
                owner = owner_ref[block // SPAN_BLK]
                oz, oy, oc = owner // 4, (owner // 2) % 2, owner % 2
                rel = (oc != c).astype(jnp.int32)
                level = jnp.where(
                    oz == z, 0, jnp.where(oz == near, 1, jnp.where(oz == inner, 2, 3))
                )
                own_column = oy == y
                direct = jnp.logical_or(level < 2, mid)
                whole = jnp.logical_and(own_column, direct)
                slot = jnp.where(jnp.logical_and(direct, level < 3), d * 2 + rel, d)
                spot = jnp.where(whole, block % SPAN_BLK, slot)
                side = jnp.where(own_column, 0, 1)
                form = jnp.where(whole, rel, jnp.where(direct, 2, 3 + side * 2 + rel))
                last_form = jnp.where(whole, 0, jnp.where(direct, 1, 2 + side))
                to = jnp.where(level == 3, 2 + rel, 1)
                index = jnp.where(level == 3, last_form, form + level * 3)
                count = plan_ref[to, d, 0]
                plan_ref[to, d, 1 + count] = index * 8 + spot
                plan_ref[to, d, 0] = count + 1
                return carry

            lax.fori_loop(0, LIST, place_block, 0)

    for d in range(2 if room else 0):

        def fetch(j, carry, d=d):
            code = plan_ref[group, d, 1 + j]
            for at, source in enumerate(sources):

                @pl.when(code // 8 == at)
                def _(source=source):
                    pltpu.make_async_copy(
                        source.at[code % 8], held.at[d, base + j], sems.at[d, j]
                    ).start()

            return carry

        lax.fori_loop(0, plan_ref[group, d, 0], fetch, 0)

    if first:
        for g in range(HALF_HEADS):
            for h in range(GROUP):
                at = (g * GROUP + h) * HEAD_SIZE
                start = pl.multiple_of(c * HALF_Q + at, HEAD_SIZE)
                rows = slice(h * BLK, (h + 1) * BLK)
                stacked_ref[g, rows] = q_ref[:, pl.ds(start, HEAD_SIZE)]
                stacked_ref[HALF_HEADS + g, rows] = pair_q_ref[:, at : at + HEAD_SIZE]
        off = pl.multiple_of(c * HALF_KV, HALF_KV)
        held[0, 0, :, :HALF_KV] = kp_ref[:, pl.ds(off, HALF_KV)]
        held[0, 0, :, HALF_KV:] = vp_ref[:, pl.ds(off, HALF_KV)]
        held[1, 0] = pair_kv_ref[...]

    def part(i, carry):
        d, g = i // HALF_HEADS, i % HALF_HEADS
        count = plan_ref[group, d, 0]
        pairs = room > 2

        if room:

            @pl.when(g == 0)
            def _():
                def arrive(j, carry):
                    pltpu.make_async_copy(
                        sources[0].at[0], held.at[d, base + j], sems.at[d, j]
                    ).wait()
                    return carry

                lax.fori_loop(0, count, arrive, 0)

                if pairs:

                    @pl.when(count % 2 == 1)
                    def _():
                        held[d, base + count] = jnp.zeros((BLK, 2 * HALF_KV), jnp.bfloat16)

        def held_of(pieces, which):
            at = pl.multiple_of(which * HALF_KV + g * HEAD_SIZE, HEAD_SIZE)
            return held[d, :pieces, :, pl.ds(at, HEAD_SIZE)].reshape(pieces * BLK, HEAD_SIZE)

        out = None
        if final:

            def out(h, value):
                at = pl.multiple_of((g * GROUP + h) * HEAD_SIZE, HEAD_SIZE)
                out_ref[d, :, pl.ds(at, HEAD_SIZE)] = value

        for even in range(0, room + 1, 2 if pairs else 1):

            @pl.when(((count + 1) // 2 * 2 if pairs else count if room else 0) == even)
            def _(even=even):
                if even == 0 and not first:
                    if not final:
                        acc_out[i] = acc_ref[i]
                        top_out[i] = top_ref[i]
                        total_out[i] = total_ref[i]
                        return
                    for h in range(GROUP):
                        rows = slice(h * BLK, (h + 1) * BLK)
                        out(h, (acc_ref[i, rows] * (1.0 / total_ref[i, rows])).astype(jnp.bfloat16))
                    return
                softmax_part(
                    even,
                    count % 2 == 1 if pairs else None,
                    first,
                    held_of,
                    stacked_ref[i],
                    s_ref,
                    p_ref,
                    None if first else (acc_ref.at[i], top_ref.at[i], total_ref.at[i]),
                    None if final else (acc_out.at[i], top_out.at[i], total_out.at[i]),
                    out,
                )

        return carry

    lax.fori_loop(0, 2 * HALF_HEADS, part, 0)


def attend(group, owner, lists, operands, sources, after):
    first, final = group == 0, group == len(GROUPS) - 1
    parts = 2 * HALF_HEADS
    room = ROOMS[group]
    pieces = room + (1 if first else 0)
    rows = GROUP * BLK
    stacked = jax.ShapeDtypeStruct((parts, rows, HEAD_SIZE), jnp.bfloat16)
    state = jax.ShapeDtypeStruct((parts, rows, HEAD_SIZE), jnp.float32)
    plan = jax.ShapeDtypeStruct((len(GROUPS), 2, 1 + LIST), jnp.int32)
    outs = [stacked, plan] if first else []
    outs += [jax.ShapeDtypeStruct((2, BLK, HALF_Q), jnp.bfloat16)] if final else [state] * 3
    used = [sources[key].reshape(-1, BLK, 2 * HALF_KV) for key in GROUPS[group]]
    keys = (pieces + 1) // 2 * BLK
    return pl.pallas_call(
        functools.partial(attend_kernel, group),
        out_shape=outs,
        in_specs=[SMEM] * 2
        + ([VMEM] * 5 if first else [VMEM] * 4 + [SMEM])
        + [ANY] * (len(used) + 1),
        out_specs=[SMEM if out is plan else VMEM for out in outs],
        scratch_shapes=[
            pltpu.VMEM((2, pieces, BLK, 2 * HALF_KV), jnp.bfloat16),
            pltpu.VMEM((rows, pieces * BLK), jnp.float32),
            pltpu.VMEM((rows, pieces * BLK), jnp.bfloat16),
            pltpu.SemaphoreType.DMA((2, max(room, 1))),
        ],
        cost_estimate=pl.CostEstimate(
            flops=4 * QUERY_HEADS * BLK * keys * HEAD_SIZE,
            bytes_accessed=4 << 20,
            transcendentals=QUERY_HEADS * BLK * keys,
        ),
        compiler_params=pltpu.CompilerParams(vmem_limit_bytes=28 << 20),
    )(owner, lists, *operands, *used, after)


def line_device(
    queries,
    prompt_keys,
    prompt_value_rows,
    document_keys,
    document_values,
    span_owner,
    block_list,
    prompt_length,
):
    first = lax.axis_index("rep") % 2 == 0

    def half(x, mine):
        width = x.shape[1] // 2
        return jnp.where(first == mine, x[:, :width], x[:, width:])

    def paired(keys, values, mine):
        return jnp.concatenate([half(keys, mine), half(values, mine)], axis=1)

    own = [paired(document_keys, document_values, True)]
    own.append(hop(paired(document_keys, document_values, False), CORE))
    outer = [hop(own[rel], OUTER) for rel in range(2)]
    inner = [hop(own[rel], INNER) for rel in range(2)]
    far = [hop(outer[rel], INNER) for rel in range(2)]

    ahead = hop(block_list, OUTER)
    both = jnp.concatenate([block_list, ahead], axis=0)
    across = hop(both, CORE)
    four = jnp.concatenate([both, across], axis=0)
    beside = hop(four, SIDE)

    def chip_lists(four, at):
        return jnp.concatenate([four[at : at + 1], four[at + 2 : at + 3]], axis=0)

    lists, side_lists = chip_lists(four, 0), chip_lists(beside, 0)
    near_lists = [chip_lists(four, 1), chip_lists(beside, 1)]
    pair_q = hop(half(queries, False), CORE)
    pair_kv = hop(paired(prompt_keys, prompt_value_rows, False), CORE)

    planes = [lambda z: z, lambda z: z ^ 1, lambda z: 3 - z, lambda z: (3 - z) ^ 1]
    spans = (own, outer, inner, far)
    sources = {(level, "whole", rel): spans[level][rel] for level in range(4) for rel in range(2)}

    def send_side(level, after):
        (side,) = slots(planes[level], span_owner, [side_lists], spans[level], (0, 1), after)
        sources[level, "side", None] = hop(side, SIDE if level < 2 else MID_SIDE)
        return side

    def send_end(level, rel, after):
        dests = near_lists + ([side_lists] if level == 3 else [])
        outs = slots(planes[level], span_owner, dests, spans[level], (rel,), after)
        sources[level, "end", rel] = hop(outs[0], END)
        sources[level, "end_side", rel] = hop(outs[1], END_SIDE)
        if level == 3:
            sources[level, "side", rel] = hop(outs[2], MID_SIDE)
        return outs[0]

    last = send_side(0, own[0])
    last = send_end(2, 0, last)
    last = send_side(1, last)
    last = send_end(2, 1, last)
    last = send_side(2, last)
    last = send_end(3, 0, last)
    operands = [queries, pair_q, prompt_keys, prompt_value_rows, pair_kv]
    stacked, plan, *state = attend(0, span_owner, lists, operands, sources, last)
    last = send_end(3, 1, state[0])
    for group in (1, 2):
        operands = [stacked, *state, plan]
        state = attend(group, span_owner, lists, operands, sources, last)
    (halves,) = attend(3, span_owner, lists, [stacked, *state, plan], sources, last)
    mine, theirs = halves[0], hop(halves[1], CORE)
    joined = jnp.where(
        first,
        jnp.concatenate([mine, theirs], axis=1),
        jnp.concatenate([theirs, mine], axis=1),
    )
    live = jnp.arange(BLK, dtype=jnp.int32) < prompt_length[0]
    return jnp.where(live[:, None], joined, jnp.zeros_like(joined))


def probs_of(query_part, key_part, visible):
    scores = jnp.einsum(
        "thd,kd->htk", query_part, key_part, preferred_element_type=jnp.float32
    ) * query_part.shape[-1] ** (-0.5)
    scores = jnp.where(visible[None], scores, -jnp.inf)
    largest = jnp.max(scores, axis=-1, keepdims=True)
    weights = jnp.exp(scores - largest)
    return (weights / jnp.sum(weights, axis=-1, keepdims=True)).astype(jnp.bfloat16)


def per_device(
    queries,
    prompt_keys,
    prompt_value_rows,
    document_keys,
    document_values,
    span_owner,
    block_list,
    prompt_length,
):
    group_width = QUERY_HEADS // KEY_VALUE_HEADS
    count = lax.axis_size("rep")
    list_len = block_list.shape[1]
    all_ranks = jnp.arange(count, dtype=jnp.int32)
    my_list = block_list[0]
    list_span = my_list // SPAN_BLK
    owners = jnp.sum(
        jnp.where(list_span[:, None] == all_ranks[None, :], span_owner[None, :], 0), axis=1
    )
    matches = owners[None, :] == all_ranks[:, None]
    request = jnp.sum(jnp.where(matches, (my_list % SPAN_BLK + 1)[None, :], 0), axis=1) - 1
    arrived = lax.all_to_all(request, "rep", split_axis=0, concat_axis=0, tiled=True)
    wanted = arrived >= 0
    inner_block = jnp.maximum(arrived, 0)

    def outgoing(source):
        blocks = source.reshape(SPAN_BLK, BLK, source.shape[1])
        picked = jnp.take(blocks, inner_block, axis=0)
        return jnp.where(wanted[:, None, None], picked, jnp.zeros_like(picked))

    def listed(received):
        return jnp.take(received, owners, axis=0).reshape(list_len * BLK, received.shape[2])

    send_keys = outgoing(document_keys)
    send_values = outgoing(document_values)
    doc_visible = jnp.ones((BLK, list_len * BLK), dtype=bool)
    got_keys, got_values = (
        lax.all_to_all(send_keys, "rep", split_axis=0, concat_axis=0, tiled=True),
        lax.all_to_all(send_values, "rep", split_axis=0, concat_axis=0, tiled=True),
    )
    query_block = 0
    seen = (query_block + 1) * BLK
    key_rows = jnp.concatenate([listed(got_keys), prompt_keys], axis=0)
    slots = jnp.arange(seen, dtype=jnp.int32)
    positions = query_block * BLK + jnp.arange(BLK, dtype=jnp.int32)
    visible = jnp.concatenate([doc_visible, slots[None, :] <= positions[:, None]], axis=1)
    row_probs = []
    for all_head_cluster in range(KEY_VALUE_HEADS):
        cols = slice(
            all_head_cluster * group_width * HEAD_SIZE,
            (all_head_cluster + 1) * group_width * HEAD_SIZE,
        )
        query_part = queries[query_block * BLK : seen, cols].reshape(BLK, group_width, HEAD_SIZE)
        row_probs.append(
            probs_of(
                query_part,
                key_rows[:, all_head_cluster * HEAD_SIZE : (all_head_cluster + 1) * HEAD_SIZE],
                visible,
            )
        )
    table = [row_probs]
    doc_value_rows = listed(got_values)
    live_rows = prompt_length[0]
    query_block = 0
    value_rows = jnp.concatenate([doc_value_rows, prompt_value_rows], axis=0)
    pieces = []
    for head_cluster in range(KEY_VALUE_HEADS):
        mixed = jnp.einsum(
            "htk,kd->thd",
            table[query_block][head_cluster],
            value_rows[:, head_cluster * HEAD_SIZE : (head_cluster + 1) * HEAD_SIZE],
            preferred_element_type=jnp.float32,
        )
        pieces.append(mixed.reshape(BLK, group_width * HEAD_SIZE))
    joined = jnp.concatenate(pieces, axis=1).astype(jnp.bfloat16)
    positions = query_block * BLK + jnp.arange(BLK, dtype=jnp.int32)
    outputs = jnp.where((positions < live_rows)[:, None], joined, jnp.zeros_like(joined))
    return outputs


def layered(*args):
    return line_device(*args)


def solution(mesh):
    line = mesh.shape["rep"] == 16
    return jax.shard_map(
        layered if line else per_device,
        mesh=mesh,
        in_specs=(
            P(("group", "rep"), None),
            P(("group", "rep"), None),
            P(("group", "rep"), None),
            P(("group", "rep"), None),
            P(("group", "rep"), None),
            P("group"),
            P(("group", "rep"), None),
            P(("group", "rep")),
        ),
        out_specs=P(("group", "rep"), None),
        check_vma=False,
    )
```

```python
import functools
import math

import jax
import jax.numpy as jnp
from jax import lax
from jax.experimental import pallas as pl
from jax.experimental.pallas import tpu as pltpu
from jax.sharding import PartitionSpec as P

QUERY_HEADS = 32
KEY_VALUE_HEADS = 4
HEAD_SIZE = 128
BLK = 128
SPAN_BLK = 4
LIST = 8
GROUP = QUERY_HEADS // KEY_VALUE_HEADS
HALF_HEADS = KEY_VALUE_HEADS // 2
HALF_KV = HALF_HEADS * HEAD_SIZE
HALF_Q = HALF_HEADS * GROUP * HEAD_SIZE
SCALE2 = math.log2(math.e) / math.sqrt(HEAD_SIZE)

GROUPS = (
    (),
    tuple(
        (level, form, rel)
        for level in range(2)
        for form, rel in (("whole", 0), ("whole", 1), ("side", None))
    )
    + ((2, "whole", 0), (2, "whole", 1), (2, "side", None))
    + ((2, "end", 0), (2, "end", 1), (2, "end_side", 0), (2, "end_side", 1)),
    ((3, "whole", 0), (3, "side", 0), (3, "end", 0), (3, "end_side", 0)),
    ((3, "whole", 1), (3, "side", 1), (3, "end", 1), (3, "end_side", 1)),
)
ROOMS = (0, 8, 2, 2)


SMEM = pl.BlockSpec(memory_space=pltpu.SMEM)
VMEM = pl.BlockSpec(memory_space=pltpu.VMEM)
ANY = pl.BlockSpec(memory_space=pl.ANY)


def rank_pairs(move):
    pairs = []
    for z in range(4):
        for y in range(2):
            for c in range(2):
                to = move(z, y, c)
                if to is not None:
                    pairs.append((z * 4 + y * 2 + c, to[0] * 4 + to[1] * 2 + to[2]))
    return pairs


CORE = rank_pairs(lambda z, y, c: (z, y, 1 - c))
SIDE = rank_pairs(lambda z, y, c: (z, 1 - y, c))
MID_SIDE = rank_pairs(lambda z, y, c: (z, 1 - y, c) if z in (1, 2) else None)
OUTER = rank_pairs(lambda z, y, c: (z ^ 1, y, c))
INNER = rank_pairs(lambda z, y, c: (3 - z, y, c) if z in (1, 2) else None)
END = rank_pairs(lambda z, y, c: (z ^ 1, y, c) if z in (1, 2) else None)
END_SIDE = rank_pairs(lambda z, y, c: (z ^ 1, 1 - y, c) if z in (1, 2) else None)


def hop(x, pairs):
    return lax.ppermute(x, "rep", pairs)


def place():
    rank = lax.axis_index("rep")
    return rank // 4, (rank // 2) % 2, rank % 2


def slot_kernel(plane_of, dests, rels, owner_ref, *refs):
    lists, refs = refs[:dests], refs[dests:]
    spans, refs = refs[: len(rels)], refs[len(rels) + 1 :]
    outs, sems = refs[:dests], refs[dests]
    z, y, c = place()
    copies = []
    for t in range(dests):
        for d in range(2):
            at = [jnp.int32(0)] * len(rels)
            for j in range(LIST):
                block = lists[t][d, j]
                owner = owner_ref[block // SPAN_BLK]
                for k, rel in enumerate(rels):
                    rank = plane_of(z) * 4 + y * 2 + (1 - c if rel else c)
                    at[k] = jnp.where(owner == rank, block % SPAN_BLK, at[k])
            for k, source in enumerate(spans):
                spot = d * len(rels) + k
                copy = pltpu.make_async_copy(
                    source.at[at[k]], outs[t].at[spot], sems.at[t * 2 * len(rels) + spot]
                )
                copy.start()
                copies.append(copy)
    for copy in copies:
        copy.wait()


def slots(plane_of, owner, lists, spans, rels, after):
    dests = len(lists)
    count = 2 * len(rels)
    shape = jax.ShapeDtypeStruct((count, BLK, 2 * HALF_KV), jnp.bfloat16)
    size = dests * count * BLK * 2 * HALF_KV * 2
    return pl.pallas_call(
        functools.partial(slot_kernel, plane_of, dests, rels),
        out_shape=[shape] * dests,
        in_specs=[SMEM] * (1 + dests) + [ANY] * (len(rels) + 1),
        out_specs=[VMEM] * dests,
        scratch_shapes=[pltpu.SemaphoreType.DMA((count * dests,))],
        cost_estimate=pl.CostEstimate(flops=0, bytes_accessed=2 * size, transcendentals=0),
        compiler_params=pltpu.CompilerParams(vmem_limit_bytes=8 << 20),
    )(owner, *lists, *[spans[rel].reshape(SPAN_BLK, BLK, 2 * HALF_KV) for rel in rels], after)


def softmax_parts(blocks, odd, prompt, held_of, query_of, s_ref, p_ref, state_in, state_out, out):
    pieces = blocks + (1 if prompt else 0)
    row = lax.broadcasted_iota(jnp.int32, (BLK, BLK), 0)
    col = lax.broadcasted_iota(jnp.int32, (BLK, BLK), 1)
    width = pieces * BLK
    for g in range(HALF_HEADS):
        s_ref[g, :, :width] = lax.dot_general(
            query_of(g),
            held_of(pieces, g, 0),
            (((1,), (1,)), ((), ())),
            preferred_element_type=jnp.float32,
        )
    for g in range(HALF_HEADS):
        before = None if state_in is None else state_in(g)
        after = None if state_out is None else state_out(g)
        scales, totals = [], []
        for h in range(GROUP):
            rows = slice(h * BLK, (h + 1) * BLK)
            parts = []
            for j in range(pieces):
                part = s_ref[g, rows, j * BLK : (j + 1) * BLK]
                if prompt and j == 0:
                    part = jnp.where(col <= row, part, -jnp.inf)
                elif j == pieces - 1 and odd is not None:
                    part = jnp.where(odd, -jnp.inf, part)
                parts.append(part)
            top = functools.reduce(jnp.maximum, parts)
            top = jnp.broadcast_to(jnp.max(top, axis=1, keepdims=True), (BLK, BLK))
            if before is not None:
                earlier = before[1][rows]
                top = jnp.maximum(top, earlier)
                scale = jnp.exp2((earlier - top) * SCALE2)
                scales.append(scale)
            total = None
            for j, part in enumerate(parts):
                weight = jnp.exp2((part - top) * SCALE2)
                total = weight if total is None else total + weight
                p_ref[g, rows, j * BLK : (j + 1) * BLK] = weight.astype(jnp.bfloat16)
            total = jnp.broadcast_to(jnp.sum(total, axis=1, keepdims=True), (BLK, BLK))
            if before is not None:
                total = total + scale * before[2][rows]
            if after is not None:
                after[1][rows] = top
                after[2][rows] = total
            else:
                totals.append(total)
        mixed = lax.dot_general(
            p_ref[g, :, :width],
            held_of(pieces, g, 1),
            (((1,), (0,)), ((), ())),
            preferred_element_type=jnp.float32,
        )
        for h in range(GROUP):
            rows = slice(h * BLK, (h + 1) * BLK)
            value = mixed[rows]
            if before is not None:
                value = value + scales[h] * before[0][rows]
            if after is not None:
                after[0][rows] = value
            else:
                out(g, h, (value * (1.0 / totals[h])).astype(jnp.bfloat16))


def attend_kernel(group, prompts, owner_ref, list_ref, *refs):
    first, final = group == 0, group == len(GROUPS) - 1
    refs = list(refs)
    if first:
        q_ref, pair_q_ref, kp_ref, vp_ref, pair_kv_ref = refs[:5]
        refs = refs[5:]
    else:
        stacked_ref, acc_ref, top_ref, total_ref, plan_ref = refs[:5]
        refs = refs[5:]
    table = GROUPS[group]
    sources, refs = refs[: len(table)], refs[len(table) + 1 :]
    if first:
        stacked_ref, plan_ref = refs[:2]
        refs = refs[2:]
    if final:
        out_ref = refs.pop(0)
    else:
        acc_out, top_out, total_out = refs[:3]
        refs = refs[3:]
    held, s_ref, p_ref, sems = refs
    room = ROOMS[group]
    base = 1 if first else 0
    z, y, c = place()
    if first:
        near = z ^ 1
        mid = jnp.logical_or(z == 1, z == 2)
        inner = jnp.where(mid, 3 - z, 3 - near)
        for d in range(2):
            for at in range(len(GROUPS)):
                plan_ref[at, d, 0] = jnp.int32(0)

            def place_block(j, carry, d=d):
                block = list_ref[d, j]
                owner = owner_ref[block // SPAN_BLK]
                oz, oy, oc = owner // 4, (owner // 2) % 2, owner % 2
                rel = (oc != c).astype(jnp.int32)
                level = jnp.where(
                    oz == z, 0, jnp.where(oz == near, 1, jnp.where(oz == inner, 2, 3))
                )
                own_column = oy == y
                direct = jnp.logical_or(level < 2, mid)
                whole = jnp.logical_and(own_column, direct)
                slot = jnp.where(jnp.logical_and(direct, level < 3), d * 2 + rel, d)
                spot = jnp.where(whole, block % SPAN_BLK, slot)
                side = jnp.where(own_column, 0, 1)
                form = jnp.where(whole, rel, jnp.where(direct, 2, 3 + side * 2 + rel))
                last_form = jnp.where(whole, 0, jnp.where(direct, 1, 2 + side))
                to = jnp.where(level == 3, 2 + rel, 1)
                index = jnp.where(level == 3, last_form, form + level * 3)
                count = plan_ref[to, d, 0]
                plan_ref[to, d, 1 + count] = index * 8 + spot
                plan_ref[to, d, 0] = count + 1
                return carry

            lax.fori_loop(0, LIST, place_block, 0)

    for d in prompts if room else ():

        def fetch(j, carry, d=d):
            code = plan_ref[group, d, 1 + j]
            for at, source in enumerate(sources):

                @pl.when(code // 8 == at)
                def _(source=source):
                    pltpu.make_async_copy(
                        source.at[code % 8], held.at[d, base + j], sems.at[d, j]
                    ).start()

            return carry

        lax.fori_loop(0, plan_ref[group, d, 0], fetch, 0)

    if first:
        for g in range(HALF_HEADS):
            for h in range(GROUP):
                at = (g * GROUP + h) * HEAD_SIZE
                start = pl.multiple_of(c * HALF_Q + at, HEAD_SIZE)
                rows = slice(h * BLK, (h + 1) * BLK)
                stacked_ref[g, rows] = q_ref[:, pl.ds(start, HEAD_SIZE)]
                stacked_ref[HALF_HEADS + g, rows] = pair_q_ref[:, at : at + HEAD_SIZE]
        off = pl.multiple_of(c * HALF_KV, HALF_KV)
        held[0, 0, :, :HALF_KV] = kp_ref[:, pl.ds(off, HALF_KV)]
        held[0, 0, :, HALF_KV:] = vp_ref[:, pl.ds(off, HALF_KV)]
        held[1, 0] = pair_kv_ref[...]

    def one_prompt(d, carry):
        count = plan_ref[group, d, 0]
        pairs = room > 2

        def arrive(j, carry):
            pltpu.make_async_copy(sources[0].at[0], held.at[d, base + j], sems.at[d, j]).wait()
            return carry

        if room:
            lax.fori_loop(0, count, arrive, 0)
        if pairs:

            @pl.when(count % 2 == 1)
            def _():
                held[d, base + count] = jnp.zeros((BLK, 2 * HALF_KV), jnp.bfloat16)

        def held_of(pieces, g, which):
            at = which * HALF_KV + g * HEAD_SIZE
            return held[d, :pieces, :, at : at + HEAD_SIZE].reshape(pieces * BLK, HEAD_SIZE)

        def state_in(g):
            i = d * HALF_HEADS + g
            return acc_ref.at[i], top_ref.at[i], total_ref.at[i]

        def state_out(g):
            i = d * HALF_HEADS + g
            return acc_out.at[i], top_out.at[i], total_out.at[i]

        def out(g, h, value):
            at = (g * GROUP + h) * HEAD_SIZE
            out_ref[:, at : at + HEAD_SIZE] = value

        for even in range(0, room + 1, 2 if pairs else 1):

            @pl.when(((count + 1) // 2 * 2 if pairs else count if room else 0) == even)
            def _(even=even):
                if even == 0 and not first:
                    for g in range(HALF_HEADS):
                        old = state_in(g)
                        if not final:
                            for to, of in zip(state_out(g), old):
                                to[...] = of[...]
                            continue
                        for h in range(GROUP):
                            rows = slice(h * BLK, (h + 1) * BLK)
                            out(g, h, (old[0][rows] * (1.0 / old[2][rows])).astype(jnp.bfloat16))
                    return
                softmax_parts(
                    even,
                    count % 2 == 1 if pairs else None,
                    first,
                    held_of,
                    lambda g: stacked_ref[d * HALF_HEADS + g],
                    s_ref,
                    p_ref,
                    None if first else state_in,
                    None if final else state_out,
                    out,
                )

        return carry

    if len(prompts) == 1:
        one_prompt(prompts[0], 0)
    else:
        lax.fori_loop(0, 2, one_prompt, 0)


def attend(group, owner, lists, operands, sources, after, prompts=(0, 1)):
    first, final = group == 0, group == len(GROUPS) - 1
    parts = 2 * HALF_HEADS
    room = ROOMS[group]
    pieces = room + (1 if first else 0)
    rows = GROUP * BLK
    stacked = jax.ShapeDtypeStruct((parts, rows, HEAD_SIZE), jnp.bfloat16)
    state = jax.ShapeDtypeStruct((parts, rows, HEAD_SIZE), jnp.float32)
    plan = jax.ShapeDtypeStruct((len(GROUPS), 2, 1 + LIST), jnp.int32)
    outs = [stacked, plan] if first else []
    outs += [jax.ShapeDtypeStruct((BLK, HALF_Q), jnp.bfloat16)] if final else [state] * 3
    used = [sources[key].reshape(-1, BLK, 2 * HALF_KV) for key in GROUPS[group]]
    keys = (pieces + 1) // 2 * BLK
    return pl.pallas_call(
        functools.partial(attend_kernel, group, prompts),
        out_shape=outs,
        in_specs=[SMEM] * 2
        + ([VMEM] * 5 if first else [VMEM] * 4 + [SMEM])
        + [ANY] * (len(used) + 1),
        out_specs=[SMEM if out is plan else VMEM for out in outs],
        scratch_shapes=[
            pltpu.VMEM((2, pieces, BLK, 2 * HALF_KV), jnp.bfloat16),
            pltpu.VMEM((HALF_HEADS, rows, pieces * BLK), jnp.float32),
            pltpu.VMEM((HALF_HEADS, rows, pieces * BLK), jnp.bfloat16),
            pltpu.SemaphoreType.DMA((2, max(room, 1))),
        ],
        cost_estimate=pl.CostEstimate(
            flops=4 * QUERY_HEADS * BLK * keys * HEAD_SIZE,
            bytes_accessed=4 << 20,
            transcendentals=QUERY_HEADS * BLK * keys,
        ),
        compiler_params=pltpu.CompilerParams(vmem_limit_bytes=28 << 20),
    )(owner, lists, *operands, *used, after)


def line_device(
    queries,
    prompt_keys,
    prompt_value_rows,
    document_keys,
    document_values,
    span_owner,
    block_list,
    prompt_length,
):
    first = lax.axis_index("rep") % 2 == 0

    def half(x, mine):
        width = x.shape[1] // 2
        return jnp.where(first == mine, x[:, :width], x[:, width:])

    def paired(keys, values, mine):
        return jnp.concatenate([half(keys, mine), half(values, mine)], axis=1)

    own = [paired(document_keys, document_values, True)]
    own.append(hop(paired(document_keys, document_values, False), CORE))
    outer = [hop(own[rel], OUTER) for rel in range(2)]
    inner = [hop(own[rel], INNER) for rel in range(2)]
    far = [hop(outer[rel], INNER) for rel in range(2)]

    ahead = hop(block_list, OUTER)
    both = jnp.concatenate([block_list, ahead], axis=0)
    across = hop(both, CORE)
    four = jnp.concatenate([both, across], axis=0)
    beside = hop(four, SIDE)

    def chip_lists(four, at):
        return jnp.concatenate([four[at : at + 1], four[at + 2 : at + 3]], axis=0)

    lists, side_lists = chip_lists(four, 0), chip_lists(beside, 0)
    near_lists = [chip_lists(four, 1), chip_lists(beside, 1)]
    live = jnp.arange(BLK, dtype=jnp.int32) < prompt_length[0]
    pair_q = hop(half(queries, False), CORE)
    pair_kv = hop(paired(prompt_keys, prompt_value_rows, False), CORE)

    planes = [lambda z: z, lambda z: z ^ 1, lambda z: 3 - z, lambda z: (3 - z) ^ 1]
    spans = (own, outer, inner, far)
    sources = {(level, "whole", rel): spans[level][rel] for level in range(4) for rel in range(2)}

    def send_side(level, after):
        (side,) = slots(planes[level], span_owner, [side_lists], spans[level], (0, 1), after)
        sources[level, "side", None] = hop(side, SIDE if level < 2 else MID_SIDE)
        return side

    def send_end(level, rel, after):
        dests = near_lists + ([side_lists] if level == 3 else [])
        outs = slots(planes[level], span_owner, dests, spans[level], (rel,), after)
        sources[level, "end", rel] = hop(outs[0], END)
        sources[level, "end_side", rel] = hop(outs[1], END_SIDE)
        if level == 3:
            sources[level, "side", rel] = hop(outs[2], MID_SIDE)
        return outs[0]

    last = send_side(0, own[0])
    operands = [queries, pair_q, prompt_keys, prompt_value_rows, pair_kv]
    stacked, plan, *state = attend(0, span_owner, lists, operands, sources, last)
    last = send_end(2, 0, state[0])
    last = send_side(1, last)
    last = send_end(2, 1, last)
    last = send_side(2, last)
    last = send_end(3, 0, last)
    last = send_end(3, 1, last)
    for group in (1, 2):
        operands = [stacked, *state, plan]
        state = attend(group, span_owner, lists, operands, sources, last)
    operands = [stacked, *state, plan]
    (theirs,) = attend(3, span_owner, lists, operands, sources, last, (1,))
    theirs = hop(theirs, CORE)
    (mine,) = attend(3, span_owner, lists, operands, sources, last, (0,))
    joined = jnp.where(
        first,
        jnp.concatenate([mine, theirs], axis=1),
        jnp.concatenate([theirs, mine], axis=1),
    )
    return jnp.where(live[:, None], joined, jnp.zeros_like(joined))


def probs_of(query_part, key_part, visible):
    scores = jnp.einsum(
        "thd,kd->htk", query_part, key_part, preferred_element_type=jnp.float32
    ) * query_part.shape[-1] ** (-0.5)
    scores = jnp.where(visible[None], scores, -jnp.inf)
    largest = jnp.max(scores, axis=-1, keepdims=True)
    weights = jnp.exp(scores - largest)
    return (weights / jnp.sum(weights, axis=-1, keepdims=True)).astype(jnp.bfloat16)


def per_device(
    queries,
    prompt_keys,
    prompt_value_rows,
    document_keys,
    document_values,
    span_owner,
    block_list,
    prompt_length,
):
    group_width = QUERY_HEADS // KEY_VALUE_HEADS
    count = lax.axis_size("rep")
    list_len = block_list.shape[1]
    all_ranks = jnp.arange(count, dtype=jnp.int32)
    my_list = block_list[0]
    list_span = my_list // SPAN_BLK
    owners = jnp.sum(
        jnp.where(list_span[:, None] == all_ranks[None, :], span_owner[None, :], 0), axis=1
    )
    matches = owners[None, :] == all_ranks[:, None]
    request = jnp.sum(jnp.where(matches, (my_list % SPAN_BLK + 1)[None, :], 0), axis=1) - 1
    arrived = lax.all_to_all(request, "rep", split_axis=0, concat_axis=0, tiled=True)
    wanted = arrived >= 0
    inner_block = jnp.maximum(arrived, 0)

    def outgoing(source):
        blocks = source.reshape(SPAN_BLK, BLK, source.shape[1])
        picked = jnp.take(blocks, inner_block, axis=0)
        return jnp.where(wanted[:, None, None], picked, jnp.zeros_like(picked))

    def listed(received):
        return jnp.take(received, owners, axis=0).reshape(list_len * BLK, received.shape[2])

    send_keys = outgoing(document_keys)
    send_values = outgoing(document_values)
    doc_visible = jnp.ones((BLK, list_len * BLK), dtype=bool)
    got_keys, got_values = (
        lax.all_to_all(send_keys, "rep", split_axis=0, concat_axis=0, tiled=True),
        lax.all_to_all(send_values, "rep", split_axis=0, concat_axis=0, tiled=True),
    )
    query_block = 0
    seen = (query_block + 1) * BLK
    key_rows = jnp.concatenate([listed(got_keys), prompt_keys], axis=0)
    slots = jnp.arange(seen, dtype=jnp.int32)
    positions = query_block * BLK + jnp.arange(BLK, dtype=jnp.int32)
    visible = jnp.concatenate([doc_visible, slots[None, :] <= positions[:, None]], axis=1)
    row_probs = []
    for all_head_cluster in range(KEY_VALUE_HEADS):
        cols = slice(
            all_head_cluster * group_width * HEAD_SIZE,
            (all_head_cluster + 1) * group_width * HEAD_SIZE,
        )
        query_part = queries[query_block * BLK : seen, cols].reshape(BLK, group_width, HEAD_SIZE)
        row_probs.append(
            probs_of(
                query_part,
                key_rows[:, all_head_cluster * HEAD_SIZE : (all_head_cluster + 1) * HEAD_SIZE],
                visible,
            )
        )
    table = [row_probs]
    doc_value_rows = listed(got_values)
    live_rows = prompt_length[0]
    query_block = 0
    value_rows = jnp.concatenate([doc_value_rows, prompt_value_rows], axis=0)
    pieces = []
    for head_cluster in range(KEY_VALUE_HEADS):
        mixed = jnp.einsum(
            "htk,kd->thd",
            table[query_block][head_cluster],
            value_rows[:, head_cluster * HEAD_SIZE : (head_cluster + 1) * HEAD_SIZE],
            preferred_element_type=jnp.float32,
        )
        pieces.append(mixed.reshape(BLK, group_width * HEAD_SIZE))
    joined = jnp.concatenate(pieces, axis=1).astype(jnp.bfloat16)
    positions = query_block * BLK + jnp.arange(BLK, dtype=jnp.int32)
    outputs = jnp.where((positions < live_rows)[:, None], joined, jnp.zeros_like(joined))
    return outputs


def layered(*args):
    return line_device(*args)


def solution(mesh):
    line = mesh.shape["rep"] == 16
    return jax.shard_map(
        layered if line else per_device,
        mesh=mesh,
        in_specs=(
            P(("group", "rep"), None),
            P(("group", "rep"), None),
            P(("group", "rep"), None),
            P(("group", "rep"), None),
            P(("group", "rep"), None),
            P("group"),
            P(("group", "rep"), None),
            P(("group", "rep")),
        ),
        out_specs=P(("group", "rep"), None),
        check_vma=False,
    )
```
